512 devices in a mesh: ctx: 64 (over z, x, core), head: 8 (over y).
Axes of the slice: x: 4, y: 8, z: 8, core: 2. Of those that a mesh axis runs over, the one named last changes fastest.
Arguments:
- query_raw: bfloat16 [8192, 2048], P('ctx', 'head'), may hold values from -6 to 6
- key_raw: bfloat16 [8192, 2048], P('ctx', 'head'), may hold values from -6 to 6
- value_raw: bfloat16 [8192, 4096], P('ctx', 'head'), may hold values from -6 to 6
- query_key_conv: bfloat16 [2, 4, 2048], P(None, None, 'head'), may hold values from -3 to 3
- value_conv: bfloat16 [4, 4096], P(None, 'head'), may hold values from -3 to 3
- output_gate: bfloat16 [8192, 4096], P('ctx', 'head'), may hold values from -6 to 6
- beta_logit: float32 [8192, 32], P('ctx', 'head')
- gate_logit: float32 [8192, 32], P('ctx', 'head')
- log_rate: float32 [32], P('head')
- norm_gain: float32 [128], replicated, may hold values from 0.5 to 2
- out_weight: bfloat16 [4096, 2048], P('head'), may hold values from -0.09375 to 0.09375
Outputs:
- mixed: bfloat16 [8192, 2048], P(('ctx', 'head'))
The draws below stay inside these ranges and needn't reach their ends.
All inputs are finite; a program needn't handle non-finite values.
Results may differ from the reference program's by a relative error of at most 0.022.
Values may be sent and summed in bfloat16 or wider, within the bound.
No kernel may reach another device: no remote copies, remote signals or barrier semaphores. Data moves between devices by JAX's collectives and lax.ppermute only.
A program may use at most 128 MiB of HBM per device.

```python
import math
import jax
import jax.numpy as jnp
from jax import lax

D = 2048
VHEADS = 32
KHEADS = 16
HDIM = 128
CONV = 4
TOK_DEV = 128
TOKENS = 8192
N_HEAD = 8


def slow_heads(key):
    sub = jax.random.fold_in(key, 11)
    share = 0.5
    return jax.random.uniform(sub, (VHEADS,), jnp.float32) < share


def draw_log_rate(key, part):
    slow = slow_heads(key)
    jitter = jax.random.uniform(jax.random.fold_in(key, 12), (VHEADS,), jnp.float32, -0.3, 0.3)
    fast_level = math.log(TOKENS / 24.0)
    return jnp.where(slow, jitter, fast_level + jitter).astype(jnp.float32)


def draw_gate_logit(key, part):
    base_offset = math.log(0.25 / TOKENS) + jax.random.uniform(jax.random.fold_in(key, 21), (TOKENS, VHEADS), jnp.float32, -1.0, 1.0)
    position_list = jax.random.randint(jax.random.fold_in(key, 22), (3, VHEADS), 0, TOKENS)
    step_count = jnp.arange(TOKENS, dtype=jnp.int32)
    token_group = jnp.any(step_count[:, None, None] == position_list[None, :, :], axis=1)
    strong_decay = jax.random.uniform(jax.random.fold_in(key, 23), (TOKENS, VHEADS), jnp.float32, -1.5, -0.5)
    return jnp.where(token_group, strong_decay, base_offset).astype(jnp.float32)


def draw_beta_logit(key, part):
    slow = slow_heads(key)
    reach = jax.random.uniform(jax.random.fold_in(key, 33), (VHEADS,), jnp.float32, math.log(2.0), math.log(12.0))
    level = math.log(HDIM / TOK_DEV) - reach
    small = level[None, :] + jax.random.uniform(jax.random.fold_in(key, 31), (TOKENS, VHEADS), jnp.float32, -1.0, 1.0)
    broad = jax.random.uniform(jax.random.fold_in(key, 32), (TOKENS, VHEADS), jnp.float32, -2.0, 2.0)
    return jnp.where(slow[None, :], small, broad).astype(jnp.float32)


def block_levels(own_key, shape, split, low, high):
    factor_of = 1.0
    for axis_at, blocks in split:
        steps = jax.random.uniform(jax.random.fold_in(jax.random.fold_in(own_key, 6), axis_at), (blocks,), jnp.float32, low / len(split), high / len(split))
        factor_of = factor_of * jnp.repeat(jnp.exp(steps), shape[axis_at] // blocks).reshape((-1,) + (1,) * (len(shape) - 1 - axis_at))
    return factor_of


def normal_values(key, shape, deviation, most, cuts=(), held_as=jnp.bfloat16):
    level = block_levels(key, shape, cuts, -0.22, 0.18) if cuts else 1.0
    array = jax.random.normal(key, shape, jnp.float32) * deviation * level
    return jnp.minimum(jnp.maximum(array, -most), most).astype(held_as)


def setup_inputs(seed: int = 0) -> dict:
    arg_keys = jax.random.split(jax.random.key(seed), 12)
    return {
        "query_raw": normal_values(arg_keys[0], (TOKENS, KHEADS * HDIM), 1.0, 6.0, ((0, 64), (1, 8))),
        "key_raw": normal_values(arg_keys[1], (TOKENS, KHEADS * HDIM), 1.0, 6.0, ((0, 64), (1, 8))),
        "value_raw": normal_values(arg_keys[2], (TOKENS, VHEADS * HDIM), 1.0, 6.0, ((0, 64), (1, 8))),
        "query_key_conv": normal_values(arg_keys[3], (2, CONV, KHEADS * HDIM), CONV ** -0.5, 3.0, ((2, 8),)),
        "value_conv": normal_values(arg_keys[4], (CONV, VHEADS * HDIM), CONV ** -0.5, 3.0, ((1, 8),)),
        "output_gate": normal_values(arg_keys[5], (TOKENS, VHEADS * HDIM), 1.0, 6.0, ((0, 64), (1, 8))),
        "beta_logit": draw_beta_logit(jax.random.fold_in(arg_keys[11], 71), 0),
        "gate_logit": draw_gate_logit(jax.random.fold_in(arg_keys[11], 71), 0),
        "log_rate": draw_log_rate(jax.random.fold_in(arg_keys[11], 71), 0),
        "norm_gain": jnp.clip(jnp.exp(jax.random.uniform(arg_keys[9], (HDIM,), jnp.float32, math.log(0.5), math.log(2.0))), 0.5, 2.0),
        "out_weight": normal_values(arg_keys[10], (VHEADS * HDIM, D), (VHEADS * HDIM) ** -0.5, 0.09375, ((0, 8),)),
    }


def conv_silu(raw_rows, taps):
    values = raw_rows.astype(jnp.float32)
    padded = jnp.pad(values, ((CONV - 1, 0), (0, 0)))
    total = jnp.zeros_like(values)
    for offset in range(CONV):
        total = total + taps[offset].astype(jnp.float32) * padded[offset:offset + values.shape[0]]
    return jax.nn.silu(total)

def unit_rows(values):
    return values / jnp.sqrt(lax.optimization_barrier(jnp.sum(values * values, axis=-1, keepdims=True)) + 1e-06)

def reference(query_raw, key_raw, value_raw, query_key_conv, value_conv, output_gate, beta_logit, gate_logit, log_rate, norm_gain, out_weight):
    highest_precision = lax.Precision.HIGHEST
    ratio = VHEADS // KHEADS
    query = unit_rows(conv_silu(query_raw, query_key_conv[0]).reshape(TOKENS, KHEADS, HDIM)) * HDIM ** (-0.5)
    key = unit_rows(conv_silu(key_raw, query_key_conv[1]).reshape(TOKENS, KHEADS, HDIM))
    value = conv_silu(value_raw, value_conv).reshape(TOKENS, VHEADS, HDIM)
    query = jnp.repeat(query, ratio, axis=1)
    key = jnp.repeat(key, ratio, axis=1)
    beta = jax.nn.sigmoid(beta_logit)
    decay = -jnp.exp(log_rate)[None, :] * jax.nn.softplus(gate_logit)

    def advance(memory_state, inputs):
        query_transposed, key_transposed, value_t, beta_t, decay_t = inputs
        memory_state = memory_state * jnp.exp(decay_t)[:, None, None]
        retrieved_value = jnp.einsum('ne,nec->nc', key_transposed, memory_state, precision=highest_precision)
        memory_state = memory_state + beta_t[:, None, None] * key_transposed[:, :, None] * (value_t - retrieved_value)[:, None, :]
        core_matrix = jnp.einsum('ne,nec->nc', query_transposed, memory_state, precision=highest_precision)
        return (memory_state, core_matrix)
    start = jnp.zeros((VHEADS, HDIM, HDIM), jnp.float32)
    _, core = lax.scan(advance, start, (query, key, value, beta, decay))
    meansq = lax.optimization_barrier(jnp.mean(core * core, axis=-1, keepdims=True))
    gate = jax.nn.silu(output_gate.reshape(TOKENS, VHEADS, HDIM).astype(jnp.float32))
    normed = (core / jnp.sqrt(meansq + 1e-06) * norm_gain * gate).astype(jnp.bfloat16)
    normed = normed.reshape(TOKENS, VHEADS * HDIM)
    group = VHEADS * HDIM // N_HEAD
    total = jnp.zeros((TOKENS, D), jnp.float32)
    for index in range(N_HEAD):
        partial_value = jnp.dot(normed[:, index * group:(index + 1) * group], out_weight[index * group:(index + 1) * group], preferred_element_type=jnp.float32)
        partial_value = lax.optimization_barrier(partial_value.astype(jnp.bfloat16))
        total = total + partial_value.astype(jnp.float32)
    return total.astype(jnp.bfloat16)
```

```python
import jax
import jax.numpy as jnp
from jax import lax
from jax.experimental import pallas as pl
from jax.experimental.pallas import tpu as pltpu
from jax.sharding import PartitionSpec as P

HDIM = 128
CONV = 4
SPAN = 128
GROUP = 4
ROW = 4
SLAB = 4
EXTRA = 16
INTERPRET = False
F32 = jnp.float32
BF16 = jnp.bfloat16
NN = (((1,), (0,)), ((), ()))
NT = (((1,), (1,)), ((), ()))
TN = (((0,), (0,)), ((), ()))


def split2(a):
    high = a.astype(BF16)
    return high, (a - high.astype(F32)).astype(BF16)


def split3(a):
    high = a.astype(BF16)
    rest = a - high.astype(F32)
    mid = rest.astype(BF16)
    return high, mid, (rest - mid.astype(F32)).astype(BF16)


def dot1(a, b, dims=NN):
    return lax.dot_general(a.astype(BF16), b.astype(BF16), dims, preferred_element_type=F32)


def dot3(a, b, dims=NN):
    a_high, a_low = split2(a)
    b_high, b_low = split2(b)
    return dot1(a_high, b_high, dims) + (dot1(a_high, b_low, dims) + dot1(a_low, b_high, dims))


def dot_mixed(a, b, dims=NN):
    b_high, b_low = split2(b)
    return dot1(a, b_high, dims) + dot1(a, b_low, dims)


def softplus(x):
    y = jnp.exp(-jnp.abs(x))
    u = 1.0 + y
    log1p = jnp.where(u == 1.0, y, jnp.log(u) * (y / jnp.where(u == 1.0, 1.0, u - 1.0)))
    return jnp.maximum(x, 0.0) + log1p


def silu(v):
    return v / (1.0 + jnp.exp(-v))


def pack_kernel(q_ref, k_ref, v_ref, beta_ref, gate_ref, rate_ref, msg_ref, *rim_refs):
    length = q_ref.shape[0]
    ratio = (v_ref.shape[1] // HDIM) // (q_ref.shape[1] // HDIM)
    beta = jax.nn.sigmoid(beta_ref[...])
    decay = -jnp.exp(rate_ref[...]) * softplus(gate_ref[...])
    lane = lax.broadcasted_iota(jnp.int32, (length, HDIM), 1)
    table = jnp.zeros((length, HDIM), F32)
    for at, values in ((0, beta), (3, decay)):
        for p, part in enumerate(split3(values)):
            part = part.astype(F32)
            for h in range(GROUP):
                table = jnp.where(lane == EXTRA * h + at + p, part[:, h : h + 1], table)
    table = table.T
    for h in range(GROUP):
        kh = h // ratio
        query = q_ref[:, kh * HDIM : (kh + 1) * HDIM]
        keyed = k_ref[:, kh * HDIM : (kh + 1) * HDIM]
        value = v_ref[:, h * HDIM : (h + 1) * HDIM]
        msg_ref[h, 0:length] = query
        msg_ref[h, length : 2 * length] = keyed
        msg_ref[h, 2 * length : 3 * length] = value
        msg_ref[h, 3 * length : 3 * length + EXTRA] = table[EXTRA * h : EXTRA * (h + 1)].astype(BF16)
        rim_refs[h][:, 0:HDIM] = query[length - 16 :]
        rim_refs[h][:, HDIM : 2 * HDIM] = keyed[length - 16 :]
        rim_refs[h][:, 2 * HDIM : 3 * HDIM] = value[length - 16 :]


def chunk_kernel(msg_ref, rim0, rim1, rim2, rim3, qk_taps_ref, v_taps_ref, map_ref, out_ref, lift_ref):
    length = SPAN
    total = GROUP * length
    place = lax.axis_index("ctx") % GROUP
    rims = [r[8:16, :].astype(F32) for r in (rim0, rim1, rim2, rim3)]
    rim = (rims[0] + rims[1]) + (rims[2] + rims[3])

    def pick(parts):
        got = parts[0]
        for i in range(1, len(parts)):
            got = jnp.where(place == i, parts[i], got)
        return got

    ratio = v_taps_ref.shape[1] // qk_taps_ref.shape[2]

    def taps_of(ref_part, repeat):
        heads = [ref_part[:, (h // repeat) * HDIM : (h // repeat + 1) * HDIM] for h in range(GROUP)]
        return pick([a.astype(F32) for a in heads])

    taps = (
        taps_of(qk_taps_ref[0], ratio),
        taps_of(qk_taps_ref[1], ratio),
        taps_of(v_taps_ref[...], 1),
    )

    def convolved(which):
        rows = [msg_ref[s, which * length : (which + 1) * length, :].astype(F32) for s in range(GROUP)]
        extended = jnp.concatenate([rim[:, which * HDIM : (which + 1) * HDIM]] + rows, axis=0)
        tap = taps[which]
        acc = tap[CONV - 1 : CONV] * extended
        for by in range(1, CONV):
            acc = acc + tap[CONV - 1 - by : CONV - by] * pltpu.roll(extended, by, 0)
        return silu(acc[8 : 8 + total])

    query = convolved(0)
    query = query * (lax.rsqrt(jnp.sum(query * query, axis=-1, keepdims=True) + 1e-06) * HDIM ** (-0.5))
    keyed = convolved(1)
    keyed = keyed * lax.rsqrt(jnp.sum(keyed * keyed, axis=-1, keepdims=True) + 1e-06)
    value = convolved(2)

    row = lax.broadcasted_iota(jnp.int32, (length, length), 0)
    col = lax.broadcasted_iota(jnp.int32, (length, length), 1)
    eye = jnp.where(row == col, 1.0, 0.0)
    lower = jnp.where(row >= col, 1.0, 0.0).astype(BF16)
    eye_b = eye.astype(BF16)
    chunks = range(GROUP)
    at = lambda a, c: a[c * length : (c + 1) * length]
    extra = [msg_ref[s, 3 * length : 3 * length + EXTRA, :] for s in chunks]
    extra_f = [e.astype(F32) for e in extra]
    beta_row = [e[0:1] + e[1:2] + e[2:3] for e in extra_f]
    extra_col = [dot1(eye_b, e, NT) for e in extra]
    beta_col = [e[:, 0:1] + e[:, 1:2] + e[:, 2:3] for e in extra_col]
    run_row = [dot1(e, lower, NT) for e in extra]
    run_col = [dot1(lower, e, NT) for e in extra]
    gamma_row = [e[3:4] + e[4:5] + e[5:6] for e in run_row]
    gamma_col = [e[:, 3:4] + e[:, 4:5] + e[:, 5:6] for e in run_col]
    gamma_end = [g[length - 1 :] for g in gamma_col]
    within = [
        jnp.where(row >= col, jnp.exp(jnp.where(row >= col, gamma_col[c] - gamma_row[c], 0.0)), 0.0)
        * beta_row[c]
        for c in chunks
    ]
    grow = [jnp.exp(g) for g in gamma_col]
    keys = [at(keyed, c) for c in chunks]
    queries = [at(query, c) for c in chunks]
    low = [jnp.where(row > col, within[c] * dot3(keys[c], keys[c], NT), 0.0) for c in chunks]
    inverse = [eye - jnp.where((row // 2) == (col // 2), low[c], 0.0) for c in chunks]
    size = 2
    while size < length:
        join = ((row // (2 * size)) == (col // (2 * size))) & ((row // size) > (col // size))
        step = [dot3(jnp.where(join, low[c], 0.0), inverse[c]) for c in chunks]
        inverse = [inverse[c] - dot3(inverse[c], step[c]) for c in chunks]
        size *= 2
    right = [jnp.concatenate([grow[c] * keys[c], at(value, c)], axis=1) for c in chunks]
    solved = [dot3(inverse[c], right[c]) for c in chunks]
    tail = [(jnp.exp(gamma_end[c] - gamma_col[c]) * beta_col[c]) * keys[c] for c in chunks]
    pushed = [dot3(tail[c], solved[c], TN) for c in chunks]
    steps = [jnp.exp(gamma_end[c]) * eye - pushed[c][:, :HDIM] for c in chunks]
    adds = [pushed[c][:, HDIM:] for c in chunks]
    before = [None]
    state = jnp.concatenate([steps[0], adds[0]], axis=1)
    for c in range(1, GROUP):
        before.append(state)
        moved = dot3(steps[c], state)
        state = jnp.concatenate([moved[:, :HDIM], moved[:, HDIM:] + adds[c]], axis=1)
    for s in range(map_ref.shape[0]):
        map_ref[s, 0:HDIM, :] = state[:, :HDIM].astype(BF16)
        map_ref[s, HDIM : 2 * HDIM, :] = state[:, HDIM:].astype(BF16)
    scores = [within[c] * dot3(queries[c], keys[c], NT) for c in chunks]
    local = [dot3(scores[c], solved[c]) for c in chunks]
    for c in chunks:
        lifted = grow[c] * queries[c] - local[c][:, :HDIM]
        own = local[c][:, HDIM:]
        if c:
            both = dot3(lifted, before[c])
            lifted = both[:, :HDIM]
            own = own + both[:, HDIM:]
        out_ref[c * length : (c + 1) * length, :] = own
        lift_ref[c * length : (c + 1) * length, :] = lifted.astype(BF16)


def chain_kernel(maps_ref, total_ref, mine_ref):
    place = (lax.axis_index("ctx") // GROUP) % ROW
    row = lax.broadcasted_iota(jnp.int32, (HDIM, 2 * HDIM), 0)
    col = lax.broadcasted_iota(jnp.int32, (HDIM, 2 * HDIM), 1)
    mine = jnp.where(row == col, 1.0, 0.0)
    state = jnp.concatenate([maps_ref[0, :HDIM, :], maps_ref[0, HDIM:, :]], axis=1).astype(F32)
    for i in range(1, ROW):
        mine = jnp.where(place == i, state, mine)
        moved = dot_mixed(maps_ref[i, :HDIM, :], state)
        state = jnp.concatenate(
            [moved[:, :HDIM], moved[:, HDIM:] + maps_ref[i, HDIM:, :].astype(F32)], axis=1
        )
    for s in range(SLAB):
        total_ref[s, :HDIM, :] = state[:, :HDIM].astype(BF16)
        total_ref[s, HDIM:, :] = state[:, HDIM:].astype(BF16)
    mine_ref[...] = mine


def finish_kernel(totals_ref, mine_ref, own_ref, lift_ref, gain_ref, normed_ref):
    place = lax.axis_index("ctx") // (GROUP * ROW)
    state = jnp.zeros((HDIM, HDIM), F32)
    got = state
    for i in range(1, SLAB):
        push = totals_ref[i - 1, HDIM:, :].astype(F32)
        state = push if i == 1 else dot_mixed(totals_ref[i - 1, :HDIM, :], state) + push
        got = jnp.where(place == i, state, got)
    start = dot3(mine_ref[:, :HDIM], got) + mine_ref[:, HDIM:]
    core = own_ref[...] + dot_mixed(lift_ref[...], start)
    mean = jnp.mean(core * core, axis=-1, keepdims=True)
    normed = (core * lax.rsqrt(mean + 1e-06) * gain_ref[...]).astype(BF16)
    for s in range(GROUP):
        normed_ref[s] = normed[s * SPAN : (s + 1) * SPAN]


def project_kernel(normed_ref, gate_ref, weight_ref, partial_ref):
    parts = []
    for h in range(GROUP):
        gate = silu(gate_ref[:, h * HDIM : (h + 1) * HDIM].astype(F32))
        parts.append((normed_ref[h].astype(F32) * gate).astype(BF16))
    left = jnp.concatenate(parts, axis=1)
    partial_ref[...] = lax.dot_general(
        left, weight_ref[...], NN, preferred_element_type=F32
    ).astype(BF16)


def call(body, outs, *args):
    return pl.pallas_call(
        body,
        out_shape=outs,
        compiler_params=pltpu.CompilerParams(vmem_limit_bytes=48 * 1024 * 1024),
        interpret=INTERPRET,
    )(*args)


def local(
    query_raw,
    key_raw,
    value_raw,
    query_key_conv,
    value_conv,
    output_gate,
    beta_logit,
    gate_logit,
    log_rate,
    norm_gain,
    out_weight,
):
    shape = jax.ShapeDtypeStruct
    devices = lax.axis_size("ctx")
    heads = lax.axis_size("head")
    length = query_raw.shape[0]
    width = out_weight.shape[1]
    near = [[GROUP * g + i for i in range(GROUP)] for g in range(devices // GROUP)]
    reach = GROUP * ROW
    rows = [
        [z * reach + GROUP * r + i for r in range(ROW)]
        for z in range(devices // reach)
        for i in range(GROUP)
    ]
    slabs = [[z * reach + i for z in range(SLAB)] for i in range(reach)]

    def trade(a, groups):
        return lax.all_to_all(a, "ctx", 0, 0, axis_index_groups=groups)

    message, *rims = call(
        pack_kernel,
        [shape((GROUP, 3 * length + EXTRA, HDIM), BF16)] + [shape((16, 3 * HDIM), BF16)] * GROUP,
        query_raw,
        key_raw,
        value_raw,
        beta_logit,
        gate_logit,
        log_rate.reshape(1, -1),
    )
    rims = [
        lax.ppermute(rim, "ctx", [(i, i + 1 + h) for i in range(GROUP - 1, devices - 1, GROUP)])
        for h, rim in enumerate(rims)
    ]
    message = trade(message, near)
    maps, own, lifted = call(
        chunk_kernel,
        [
            shape((ROW, 2 * HDIM, HDIM), BF16),
            shape((GROUP * SPAN, HDIM), F32),
            shape((GROUP * SPAN, HDIM), BF16),
        ],
        message,
        *rims,
        query_key_conv,
        value_conv,
    )
    maps = trade(maps, rows)
    totals, mine = call(
        chain_kernel,
        [shape((SLAB, 2 * HDIM, HDIM), BF16), shape((HDIM, 2 * HDIM), F32)],
        maps,
    )
    totals = trade(totals, slabs)
    normed = call(
        finish_kernel,
        shape((GROUP, SPAN, HDIM), BF16),
        totals,
        mine,
        own,
        lifted,
        norm_gain.reshape(1, -1),
    )
    normed = trade(normed, near)
    partial = call(project_kernel, shape((length, width), BF16), normed, output_gate, out_weight)
    partial = lax.all_to_all(partial.reshape(heads, length // heads, width), "head", 0, 0)
    return jnp.sum(partial.astype(F32), axis=0).astype(BF16)


def solution(mesh):
    in_specs = (
        P("ctx", "head"),
        P("ctx", "head"),
        P("ctx", "head"),
        P(None, None, "head"),
        P(None, "head"),
        P("ctx", "head"),
        P("ctx", "head"),
        P("ctx", "head"),
        P("head"),
        P(),
        P("head", None),
    )
    out_specs = P(("ctx", "head"), None)
    return jax.shard_map(local, mesh=mesh, in_specs=in_specs, out_specs=out_specs, check_vma=False)
```

```python
import jax
import jax.numpy as jnp
from jax import lax
from jax.experimental import pallas as pl
from jax.experimental.pallas import tpu as pltpu
from jax.sharding import PartitionSpec as P

HDIM = 128
CONV = 4
SPAN = 128
GROUP = 4
ROW = 4
SLAB = 4
EXTRA = 16
INTERPRET = False
F32 = jnp.float32
BF16 = jnp.bfloat16
NN = (((1,), (0,)), ((), ()))
NT = (((1,), (1,)), ((), ()))
TN = (((0,), (0,)), ((), ()))


def split2(a):
    high = a.astype(BF16)
    return high, (a - high.astype(F32)).astype(BF16)


def split3(a):
    high = a.astype(BF16)
    rest = a - high.astype(F32)
    mid = rest.astype(BF16)
    return high, mid, (rest - mid.astype(F32)).astype(BF16)


def dot1(a, b, dims=NN):
    return lax.dot_general(a.astype(BF16), b.astype(BF16), dims, preferred_element_type=F32)


def dot3(a, b, dims=NN):
    a_high, a_low = split2(a)
    b_high, b_low = split2(b)
    return dot1(a_high, b_high, dims) + (dot1(a_high, b_low, dims) + dot1(a_low, b_high, dims))


def dot_mixed(a, b, dims=NN):
    b_high, b_low = split2(b)
    return dot1(a, b_high, dims) + dot1(a, b_low, dims)


def softplus(x):
    y = jnp.exp(-jnp.abs(x))
    u = 1.0 + y
    log1p = jnp.where(u == 1.0, y, jnp.log(u) * (y / jnp.where(u == 1.0, 1.0, u - 1.0)))
    return jnp.maximum(x, 0.0) + log1p


def silu(v):
    return v / (1.0 + jnp.exp(-v))


def pack_kernel(
    q_hbm, k_hbm, v_hbm, qk_taps_hbm, v_taps_hbm, beta_hbm, gate_hbm, rate_ref, msg_ref, taps_ref,
    rim0, rim1, rim2, rim3, q_ref, k_ref, v_ref, qk_taps_ref, v_taps_ref, beta_ref, gate_ref, sems,
):
    rim_refs = (rim0, rim1, rim2, rim3)
    sources = (beta_hbm, gate_hbm, q_hbm, k_hbm, v_hbm, qk_taps_hbm, v_taps_hbm)
    targets = (beta_ref, gate_ref, q_ref, k_ref, v_ref, qk_taps_ref, v_taps_ref)
    copies = [pltpu.make_async_copy(x, y, sems.at[i]) for i, (x, y) in enumerate(zip(sources, targets))]
    for c in copies:
        c.start()
    length = q_ref.shape[0]
    ratio = v_ref.shape[1] // q_ref.shape[1]
    for c in copies[:2]:
        c.wait()
    beta = split3(jax.nn.sigmoid(beta_ref[...]))
    soft = softplus(gate_ref[...])
    head_row = lax.broadcasted_iota(jnp.int32, soft.shape, 0)
    rate = jnp.zeros(soft.shape, F32)
    for h in range(GROUP):
        rate = jnp.where(head_row == h, rate_ref[h], rate)
    decay = split3(-jnp.exp(rate) * soft)
    blank = jnp.zeros((EXTRA - 6, length), F32)
    for h in range(GROUP):
        rows = [p[h : h + 1].astype(F32) for p in beta + decay] + [blank]
        msg_ref[h, 3 * length :] = jnp.concatenate(rows, axis=0).astype(BF16)
    for c in copies[2:]:
        c.wait()
    for h in range(GROUP):
        kh = h // ratio
        query = q_ref[:, kh * HDIM : (kh + 1) * HDIM]
        keyed = k_ref[:, kh * HDIM : (kh + 1) * HDIM]
        value = v_ref[:, h * HDIM : (h + 1) * HDIM]
        msg_ref[h, 0:length] = query
        msg_ref[h, length : 2 * length] = keyed
        msg_ref[h, 2 * length : 3 * length] = value
        rim_refs[h][:, 0:HDIM] = query[length - 16 :]
        rim_refs[h][:, HDIM : 2 * HDIM] = keyed[length - 16 :]
        rim_refs[h][:, 2 * HDIM : 3 * HDIM] = value[length - 16 :]
    place = lax.axis_index("ctx") % GROUP

    def pick(taps, heads):
        parts = [taps[:, i * HDIM : (i + 1) * HDIM] for i in heads]
        got = parts[0]
        for i in range(1, GROUP):
            got = jnp.where(place == i, parts[i], got)
        return got

    key_heads = [h // ratio for h in range(GROUP)]
    taps_ref[0:4, :] = pick(qk_taps_ref[0].astype(F32), key_heads)
    taps_ref[4:8, :] = pick(qk_taps_ref[1].astype(F32), key_heads)
    taps_ref[8:12, :] = pick(v_taps_ref[...].astype(F32), range(GROUP))
    taps_ref[12:16, :] = jnp.zeros((4, HDIM), F32)


def chunk_kernel(msg_ref, taps_ref, rim0, rim1, rim2, rim3, map_ref, out_ref, lift_ref):
    length = SPAN
    total = GROUP * length
    rims = [r[8:16, :].astype(F32) for r in (rim0, rim1, rim2, rim3)]
    rim = (rims[0] + rims[1]) + (rims[2] + rims[3])

    def convolved(which):
        rows = [msg_ref[s, which * length : (which + 1) * length, :].astype(F32) for s in range(GROUP)]
        extended = jnp.concatenate([rim[:, which * HDIM : (which + 1) * HDIM]] + rows, axis=0)
        tap = taps_ref[4 * which : 4 * which + 4, :]
        acc = tap[CONV - 1 : CONV] * extended
        for by in range(1, CONV):
            acc = acc + tap[CONV - 1 - by : CONV - by] * pltpu.roll(extended, by, 0)
        return silu(acc[8 : 8 + total])

    query = convolved(0)
    query = query * (lax.rsqrt(jnp.sum(query * query, axis=-1, keepdims=True) + 1e-06) * HDIM ** (-0.5))
    keyed = convolved(1)
    keyed = keyed * lax.rsqrt(jnp.sum(keyed * keyed, axis=-1, keepdims=True) + 1e-06)
    value = convolved(2)

    row = lax.broadcasted_iota(jnp.int32, (length, length), 0)
    col = lax.broadcasted_iota(jnp.int32, (length, length), 1)
    eye = jnp.where(row == col, 1.0, 0.0)
    lower = jnp.where(row >= col, 1.0, 0.0).astype(BF16)
    eye_b = eye.astype(BF16)
    chunks = range(GROUP)
    at = lambda a, c: a[c * length : (c + 1) * length]
    extra = [msg_ref[s, 3 * length : 3 * length + EXTRA, :] for s in chunks]
    extra_f = [e.astype(F32) for e in extra]
    beta_row = [e[0:1] + e[1:2] + e[2:3] for e in extra_f]
    extra_col = [dot1(eye_b, e, NT) for e in extra]
    beta_col = [e[:, 0:1] + e[:, 1:2] + e[:, 2:3] for e in extra_col]
    run_row = [dot1(e, lower, NT) for e in extra]
    run_col = [dot1(lower, e, NT) for e in extra]
    gamma_row = [e[3:4] + e[4:5] + e[5:6] for e in run_row]
    gamma_col = [e[:, 3:4] + e[:, 4:5] + e[:, 5:6] for e in run_col]
    gamma_end = [g[length - 1 :] for g in gamma_col]
    within = [
        jnp.where(row >= col, jnp.exp(jnp.where(row >= col, gamma_col[c] - gamma_row[c], 0.0)), 0.0)
        * beta_row[c]
        for c in chunks
    ]
    grow = [jnp.exp(g) for g in gamma_col]
    keys = [at(keyed, c) for c in chunks]
    queries = [at(query, c) for c in chunks]
    low = [jnp.where(row > col, within[c] * dot3(keys[c], keys[c], NT), 0.0) for c in chunks]
    inverse = [eye - jnp.where((row // 2) == (col // 2), low[c], 0.0) for c in chunks]
    size = 2
    while size < length:
        join = ((row // (2 * size)) == (col // (2 * size))) & ((row // size) > (col // size))
        step = [dot3(jnp.where(join, low[c], 0.0), inverse[c]) for c in chunks]
        inverse = [inverse[c] - dot3(inverse[c], step[c]) for c in chunks]
        size *= 2
    right = [jnp.concatenate([grow[c] * keys[c], at(value, c)], axis=1) for c in chunks]
    solved = [dot3(inverse[c], right[c]) for c in chunks]
    tail = [(jnp.exp(gamma_end[c] - gamma_col[c]) * beta_col[c]) * keys[c] for c in chunks]
    pushed = [dot3(tail[c], solved[c], TN) for c in chunks]
    steps = [jnp.exp(gamma_end[c]) * eye - pushed[c][:, :HDIM] for c in chunks]
    adds = [pushed[c][:, HDIM:] for c in chunks]
    before = [None]
    state = jnp.concatenate([steps[0], adds[0]], axis=1)
    for c in range(1, GROUP):
        before.append(state)
        moved = dot3(steps[c], state)
        state = jnp.concatenate([moved[:, :HDIM], moved[:, HDIM:] + adds[c]], axis=1)
    for s in range(map_ref.shape[0]):
        map_ref[s, 0:HDIM, :] = state[:, :HDIM].astype(BF16)
        map_ref[s, HDIM : 2 * HDIM, :] = state[:, HDIM:].astype(BF16)
    scores = [within[c] * dot3(queries[c], keys[c], NT) for c in chunks]
    local = [dot3(scores[c], solved[c]) for c in chunks]
    for c in chunks:
        lifted = grow[c] * queries[c] - local[c][:, :HDIM]
        own = local[c][:, HDIM:]
        if c:
            both = dot3(lifted, before[c])
            lifted = both[:, :HDIM]
            own = own + both[:, HDIM:]
        out_ref[c * length : (c + 1) * length, :] = own
        lift_ref[c * length : (c + 1) * length, :] = lifted.astype(BF16)


def chain_kernel(maps_ref, total_ref, mine_ref):
    place = (lax.axis_index("ctx") // GROUP) % ROW
    row = lax.broadcasted_iota(jnp.int32, (HDIM, 2 * HDIM), 0)
    col = lax.broadcasted_iota(jnp.int32, (HDIM, 2 * HDIM), 1)
    mine = jnp.where(row == col, 1.0, 0.0)
    state = jnp.concatenate([maps_ref[0, :HDIM, :], maps_ref[0, HDIM:, :]], axis=1).astype(F32)
    for i in range(1, ROW):
        mine = jnp.where(place == i, state, mine)
        moved = dot_mixed(maps_ref[i, :HDIM, :], state)
        state = jnp.concatenate(
            [moved[:, :HDIM], moved[:, HDIM:] + maps_ref[i, HDIM:, :].astype(F32)], axis=1
        )
    for s in range(SLAB):
        total_ref[s, :HDIM, :] = state[:, :HDIM].astype(BF16)
        total_ref[s, HDIM:, :] = state[:, HDIM:].astype(BF16)
    mine_ref[...] = mine


def finish_kernel(totals_ref, mine_ref, own_ref, lift_ref, gain_ref, normed_ref):
    place = lax.axis_index("ctx") // (GROUP * ROW)
    state = jnp.zeros((HDIM, HDIM), F32)
    got = state
    for i in range(1, SLAB):
        push = totals_ref[i - 1, HDIM:, :].astype(F32)
        state = push if i == 1 else dot_mixed(totals_ref[i - 1, :HDIM, :], state) + push
        got = jnp.where(place == i, state, got)
    start = dot3(mine_ref[:, :HDIM], got) + mine_ref[:, HDIM:]
    core = own_ref[...] + dot_mixed(lift_ref[...], start)
    mean = jnp.mean(core * core, axis=-1, keepdims=True)
    normed = (core * lax.rsqrt(mean + 1e-06) * gain_ref[...]).astype(BF16)
    for s in range(GROUP):
        normed_ref[s] = normed[s * SPAN : (s + 1) * SPAN]


def project_kernel(normed_ref, gate_ref, weight_ref, partial_ref):
    parts = []
    for h in range(GROUP):
        gate = silu(gate_ref[:, h * HDIM : (h + 1) * HDIM].astype(F32))
        parts.append((normed_ref[h].astype(F32) * gate).astype(BF16))
    left = jnp.concatenate(parts, axis=1)
    partial_ref[...] = lax.dot_general(
        left, weight_ref[...], NN, preferred_element_type=F32
    ).astype(BF16)


def call(body, outs, *args, **more):
    return pl.pallas_call(
        body,
        out_shape=outs,
        compiler_params=pltpu.CompilerParams(vmem_limit_bytes=32 * 1024 * 1024),
        interpret=pltpu.InterpretParams() if INTERPRET else False,
        **more,
    )(*args)


def in_hbm(a):
    return a if INTERPRET else pltpu.with_memory_space_constraint(a, pltpu.HBM)


def local(
    query_raw,
    key_raw,
    value_raw,
    query_key_conv,
    value_conv,
    output_gate,
    beta_logit,
    gate_logit,
    log_rate,
    norm_gain,
    out_weight,
):
    shape = jax.ShapeDtypeStruct
    devices = lax.axis_size("ctx")
    heads = lax.axis_size("head")
    length = query_raw.shape[0]
    width = out_weight.shape[1]
    near = [[GROUP * g + i for i in range(GROUP)] for g in range(devices // GROUP)]
    reach = GROUP * ROW
    rows = [
        [z * reach + GROUP * r + i for r in range(ROW)]
        for z in range(devices // reach)
        for i in range(GROUP)
    ]
    slabs = [[z * reach + i for z in range(SLAB)] for i in range(reach)]

    def trade(a, groups):
        return lax.all_to_all(a, "ctx", 0, 0, axis_index_groups=groups)

    raw = (query_raw, key_raw, value_raw, query_key_conv, value_conv, beta_logit.T, gate_logit.T)
    fetched = [pltpu.VMEM(raw[i].shape, raw[i].dtype) for i in range(len(raw))]
    message, taps, *rims = call(
        pack_kernel,
        [shape((GROUP, 3 * length + EXTRA, HDIM), BF16), shape((16, HDIM), F32)]
        + [shape((16, 3 * HDIM), BF16)] * GROUP,
        *[in_hbm(a) for a in raw],
        in_hbm(log_rate),
        in_specs=[pl.BlockSpec(memory_space=pltpu.HBM)] * len(raw) + [pl.BlockSpec(memory_space=pltpu.SMEM)],
        scratch_shapes=fetched + [pltpu.SemaphoreType.DMA((len(raw),))],
    )
    rims = [
        lax.ppermute(rim, "ctx", [(i, i + 1 + h) for i in range(GROUP - 1, devices - 1, GROUP)])
        for h, rim in enumerate(rims)
    ]
    message = trade(message, near)
    maps, own, lifted = call(
        chunk_kernel,
        [
            shape((ROW, 2 * HDIM, HDIM), BF16),
            shape((GROUP * SPAN, HDIM), F32),
            shape((GROUP * SPAN, HDIM), BF16),
        ],
        message,
        taps,
        *rims,
    )
    maps = trade(maps, rows)
    totals, mine = call(
        chain_kernel,
        [shape((SLAB, 2 * HDIM, HDIM), BF16), shape((HDIM, 2 * HDIM), F32)],
        maps,
    )
    totals = trade(totals, slabs)
    normed = call(
        finish_kernel,
        shape((GROUP, SPAN, HDIM), BF16),
        totals,
        mine,
        own,
        lifted,
        norm_gain.reshape(1, -1),
    )
    normed = trade(normed, near)
    partial = call(project_kernel, shape((length, width), BF16), normed, output_gate, out_weight)
    partial = lax.all_to_all(partial.reshape(heads, length // heads, width), "head", 0, 0)
    return jnp.sum(partial.astype(F32), axis=0).astype(BF16)


def solution(mesh):
    in_specs = (
        P("ctx", "head"),
        P("ctx", "head"),
        P("ctx", "head"),
        P(None, None, "head"),
        P(None, "head"),
        P("ctx", "head"),
        P("ctx", "head"),
        P("ctx", "head"),
        P("head"),
        P(),
        P("head", None),
    )
    out_specs = P(("ctx", "head"), None)
    return jax.shard_map(local, mesh=mesh, in_specs=in_specs, out_specs=out_specs, check_vma=False)
```

```python
import jax
import jax.numpy as jnp
from jax import lax
from jax.experimental import pallas as pl
from jax.experimental.pallas import tpu as pltpu
from jax.sharding import PartitionSpec as P

HDIM = 128
CONV = 4
SPAN = 128
GROUP = 4
ROW = 4
SLAB = 4
EXTRA = 16
INTERPRET = False
F32 = jnp.float32
BF16 = jnp.bfloat16
NN = (((1,), (0,)), ((), ()))
NT = (((1,), (1,)), ((), ()))
TN = (((0,), (0,)), ((), ()))


def split2(a):
    high = a.astype(BF16)
    return high, (a - high.astype(F32)).astype(BF16)


def split3(a):
    high = a.astype(BF16)
    rest = a - high.astype(F32)
    mid = rest.astype(BF16)
    return high, mid, (rest - mid.astype(F32)).astype(BF16)


def dot1(a, b, dims=NN):
    return lax.dot_general(a.astype(BF16), b.astype(BF16), dims, preferred_element_type=F32)


def dot3(a, b, dims=NN):
    a_high, a_low = split2(a)
    b_high, b_low = split2(b)
    return dot1(a_high, b_high, dims) + (dot1(a_high, b_low, dims) + dot1(a_low, b_high, dims))


def dot_mixed(a, b, dims=NN):
    b_high, b_low = split2(b)
    return dot1(a, b_high, dims) + dot1(a, b_low, dims)


def softplus(x):
    y = jnp.exp(-jnp.abs(x))
    u = 1.0 + y
    log1p = jnp.where(u == 1.0, y, jnp.log(u) * (y / jnp.where(u == 1.0, 1.0, u - 1.0)))
    return jnp.maximum(x, 0.0) + log1p


def silu(v):
    return v / (1.0 + jnp.exp(-v))


def pack_kernel(
    q_hbm, k_hbm, v_hbm, qk_taps_hbm, v_taps_hbm, beta_hbm, gate_hbm, rate_ref, msg_ref, taps_ref,
    rim0, rim1, rim2, rim3, q_ref, k_ref, v_ref, qk_taps_ref, v_taps_ref, beta_ref, gate_ref, sems,
):
    rim_refs = (rim0, rim1, rim2, rim3)
    sources = (beta_hbm, gate_hbm, q_hbm, k_hbm, v_hbm, qk_taps_hbm, v_taps_hbm)
    targets = (beta_ref, gate_ref, q_ref, k_ref, v_ref, qk_taps_ref, v_taps_ref)
    copies = [pltpu.make_async_copy(x, y, sems.at[i]) for i, (x, y) in enumerate(zip(sources, targets))]
    for c in copies:
        c.start()
    length = q_ref.shape[0]
    ratio = v_ref.shape[1] // q_ref.shape[1]
    for c in copies[:2]:
        c.wait()
    beta = split3(jax.nn.sigmoid(beta_ref[...]))
    soft = softplus(gate_ref[...])
    head_row = lax.broadcasted_iota(jnp.int32, soft.shape, 0)
    rate = jnp.zeros(soft.shape, F32)
    for h in range(GROUP):
        rate = jnp.where(head_row == h, rate_ref[h], rate)
    decay = split3(-jnp.exp(rate) * soft)
    blank = jnp.zeros((EXTRA - 6, length), F32)
    for h in range(GROUP):
        rows = [p[h : h + 1].astype(F32) for p in beta + decay] + [blank]
        msg_ref[h, 3 * length :] = jnp.concatenate(rows, axis=0).astype(BF16)
    for c in copies[2:]:
        c.wait()
    for h in range(GROUP):
        kh = h // ratio
        query = q_ref[:, kh * HDIM : (kh + 1) * HDIM]
        keyed = k_ref[:, kh * HDIM : (kh + 1) * HDIM]
        value = v_ref[:, h * HDIM : (h + 1) * HDIM]
        msg_ref[h, 0:length] = query
        msg_ref[h, length : 2 * length] = keyed
        msg_ref[h, 2 * length : 3 * length] = value
        rim_refs[h][:, 0:HDIM] = query[length - 16 :]
        rim_refs[h][:, HDIM : 2 * HDIM] = keyed[length - 16 :]
        rim_refs[h][:, 2 * HDIM : 3 * HDIM] = value[length - 16 :]
    place = lax.axis_index("ctx") % GROUP

    def pick(taps, heads):
        parts = [taps[:, i * HDIM : (i + 1) * HDIM] for i in heads]
        got = parts[0]
        for i in range(1, GROUP):
            got = jnp.where(place == i, parts[i], got)
        return got

    key_heads = [h // ratio for h in range(GROUP)]
    taps_ref[0:4, :] = pick(qk_taps_ref[0].astype(F32), key_heads)
    taps_ref[4:8, :] = pick(qk_taps_ref[1].astype(F32), key_heads)
    taps_ref[8:12, :] = pick(v_taps_ref[...].astype(F32), range(GROUP))
    taps_ref[12:16, :] = jnp.zeros((4, HDIM), F32)


def chunk_kernel(msg_ref, taps_ref, rim0, rim1, rim2, rim3, map_ref, out_ref, lift_ref):
    length = SPAN
    total = GROUP * length
    rims = [r[8:16, :].astype(F32) for r in (rim0, rim1, rim2, rim3)]
    rim = (rims[0] + rims[1]) + (rims[2] + rims[3])

    def convolved(which):
        rows = [msg_ref[s, which * length : (which + 1) * length, :].astype(F32) for s in range(GROUP)]
        extended = jnp.concatenate([rim[:, which * HDIM : (which + 1) * HDIM]] + rows, axis=0)
        tap = taps_ref[4 * which : 4 * which + 4, :]
        acc = tap[CONV - 1 : CONV] * extended
        for by in range(1, CONV):
            acc = acc + tap[CONV - 1 - by : CONV - by] * pltpu.roll(extended, by, 0)
        return silu(acc[8 : 8 + total])

    query = convolved(0)
    query = query * (lax.rsqrt(jnp.sum(query * query, axis=-1, keepdims=True) + 1e-06) * HDIM ** (-0.5))
    keyed = convolved(1)
    keyed = keyed * lax.rsqrt(jnp.sum(keyed * keyed, axis=-1, keepdims=True) + 1e-06)
    value = convolved(2)

    row = lax.broadcasted_iota(jnp.int32, (length, length), 0)
    col = lax.broadcasted_iota(jnp.int32, (length, length), 1)
    eye = jnp.where(row == col, 1.0, 0.0)
    lower = jnp.where(row >= col, 1.0, 0.0).astype(BF16)
    eye_b = eye.astype(BF16)
    chunks = range(GROUP)
    at = lambda a, c: a[c * length : (c + 1) * length]
    extra = [msg_ref[s, 3 * length : 3 * length + EXTRA, :] for s in chunks]
    extra_f = [e.astype(F32) for e in extra]
    beta_row = [e[0:1] + e[1:2] + e[2:3] for e in extra_f]
    extra_col = [dot1(eye_b, e, NT) for e in extra]
    beta_col = [e[:, 0:1] + e[:, 1:2] + e[:, 2:3] for e in extra_col]
    run_row = [dot1(e, lower, NT) for e in extra]
    run_col = [dot1(lower, e, NT) for e in extra]
    gamma_row = [e[3:4] + e[4:5] + e[5:6] for e in run_row]
    gamma_col = [e[:, 3:4] + e[:, 4:5] + e[:, 5:6] for e in run_col]
    gamma_end = [g[length - 1 :] for g in gamma_col]
    within = [
        jnp.where(row >= col, jnp.exp(jnp.where(row >= col, gamma_col[c] - gamma_row[c], 0.0)), 0.0)
        * beta_row[c]
        for c in chunks
    ]
    grow = [jnp.exp(g) for g in gamma_col]
    keys = [at(keyed, c) for c in chunks]
    queries = [at(query, c) for c in chunks]
    low = [jnp.where(row > col, within[c] * dot3(keys[c], keys[c], NT), 0.0) for c in chunks]
    inverse = [eye - jnp.where((row // 2) == (col // 2), low[c], 0.0) for c in chunks]
    size = 2
    while size < length:
        join = ((row // (2 * size)) == (col // (2 * size))) & ((row // size) > (col // size))
        step = [dot3(jnp.where(join, low[c], 0.0), inverse[c]) for c in chunks]
        inverse = [inverse[c] - dot3(inverse[c], step[c]) for c in chunks]
        size *= 2
    right = [jnp.concatenate([grow[c] * keys[c], at(value, c)], axis=1) for c in chunks]
    solved = [dot3(inverse[c], right[c]) for c in chunks]
    tail = [(jnp.exp(gamma_end[c] - gamma_col[c]) * beta_col[c]) * keys[c] for c in chunks]
    pushed = [dot3(tail[c], solved[c], TN) for c in chunks]
    steps = [jnp.exp(gamma_end[c]) * eye - pushed[c][:, :HDIM] for c in chunks]
    adds = [pushed[c][:, HDIM:] for c in chunks]
    before = [None]
    state = jnp.concatenate([steps[0], adds[0]], axis=1)
    for c in range(1, GROUP):
        before.append(state)
        moved = dot3(steps[c], state)
        state = jnp.concatenate([moved[:, :HDIM], moved[:, HDIM:] + adds[c]], axis=1)
    for s in range(map_ref.shape[0]):
        map_ref[s, 0:HDIM, :] = state[:, :HDIM].astype(BF16)
        map_ref[s, HDIM : 2 * HDIM, :] = state[:, HDIM:].astype(BF16)
    scores = [within[c] * dot3(queries[c], keys[c], NT) for c in chunks]
    local = [dot3(scores[c], solved[c]) for c in chunks]
    for c in chunks:
        lifted = grow[c] * queries[c] - local[c][:, :HDIM]
        own = local[c][:, HDIM:]
        if c:
            both = dot3(lifted, before[c])
            lifted = both[:, :HDIM]
            own = own + both[:, HDIM:]
        out_ref[c * length : (c + 1) * length, :] = own
        lift_ref[c * length : (c + 1) * length, :] = lifted.astype(BF16)


def chain_kernel(maps_ref, step_ref, add_ref, mine_ref):
    place = (lax.axis_index("ctx") // GROUP) % ROW
    row = lax.broadcasted_iota(jnp.int32, (HDIM, 2 * HDIM), 0)
    col = lax.broadcasted_iota(jnp.int32, (HDIM, 2 * HDIM), 1)
    mine = jnp.where(row == col, 1.0, 0.0)
    state = jnp.concatenate([maps_ref[0, :HDIM, :], maps_ref[0, HDIM:, :]], axis=1).astype(F32)
    for i in range(1, ROW):
        mine = jnp.where(place == i, state, mine)
        moved = dot_mixed(maps_ref[i, :HDIM, :], state)
        state = jnp.concatenate(
            [moved[:, :HDIM], moved[:, HDIM:] + maps_ref[i, HDIM:, :].astype(F32)], axis=1
        )
    step_ref[...] = state[:, :HDIM].astype(BF16)
    add_ref[...] = state[:, HDIM:].astype(BF16)
    mine_ref[...] = mine


def relay_kernel(step_ref, add_ref, *refs):
    state = refs[0][...]
    for r in refs[1:-1]:
        state = state + r[...]
    refs[-1][...] = (dot1(step_ref[...], state) + add_ref[...].astype(F32)).astype(BF16)


def finish_kernel(first_ref, second_ref, third_ref, mine_ref, own_ref, lift_ref, gain_ref, normed_ref):
    got = first_ref[...].astype(F32) + second_ref[...].astype(F32) + third_ref[...].astype(F32)
    start = dot3(mine_ref[:, :HDIM], got) + mine_ref[:, HDIM:]
    core = own_ref[...] + dot_mixed(lift_ref[...], start)
    mean = jnp.mean(core * core, axis=-1, keepdims=True)
    normed = (core * lax.rsqrt(mean + 1e-06) * gain_ref[...]).astype(BF16)
    for s in range(GROUP):
        normed_ref[s] = normed[s * SPAN : (s + 1) * SPAN]


def project_kernel(normed_ref, gate_ref, weight_ref, partial_ref):
    parts = []
    for h in range(GROUP):
        gate = silu(gate_ref[:, h * HDIM : (h + 1) * HDIM].astype(F32))
        parts.append((normed_ref[h].astype(F32) * gate).astype(BF16))
    left = jnp.concatenate(parts, axis=1)
    partial_ref[...] = lax.dot_general(
        left, weight_ref[...], NN, preferred_element_type=F32
    ).astype(BF16)


def call(body, outs, *args, **more):
    return pl.pallas_call(
        body,
        out_shape=outs,
        compiler_params=pltpu.CompilerParams(vmem_limit_bytes=32 * 1024 * 1024),
        interpret=pltpu.InterpretParams() if INTERPRET else False,
        **more,
    )(*args)


def in_hbm(a):
    return a if INTERPRET else pltpu.with_memory_space_constraint(a, pltpu.HBM)


def local(
    query_raw,
    key_raw,
    value_raw,
    query_key_conv,
    value_conv,
    output_gate,
    beta_logit,
    gate_logit,
    log_rate,
    norm_gain,
    out_weight,
):
    shape = jax.ShapeDtypeStruct
    devices = lax.axis_size("ctx")
    heads = lax.axis_size("head")
    length = query_raw.shape[0]
    width = out_weight.shape[1]
    near = [[GROUP * g + i for i in range(GROUP)] for g in range(devices // GROUP)]
    reach = GROUP * ROW
    rows = [
        [z * reach + GROUP * r + i for r in range(ROW)]
        for z in range(devices // reach)
        for i in range(GROUP)
    ]

    def trade(a, groups):
        return lax.all_to_all(a, "ctx", 0, 0, axis_index_groups=groups)

    raw = (query_raw, key_raw, value_raw, query_key_conv, value_conv, beta_logit.T, gate_logit.T)
    fetched = [pltpu.VMEM(raw[i].shape, raw[i].dtype) for i in range(len(raw))]
    message, taps, *rims = call(
        pack_kernel,
        [shape((GROUP, 3 * length + EXTRA, HDIM), BF16), shape((16, HDIM), F32)]
        + [shape((16, 3 * HDIM), BF16)] * GROUP,
        *[in_hbm(a) for a in raw],
        in_hbm(log_rate),
        in_specs=[pl.BlockSpec(memory_space=pltpu.HBM)] * len(raw) + [pl.BlockSpec(memory_space=pltpu.SMEM)],
        scratch_shapes=fetched + [pltpu.SemaphoreType.DMA((len(raw),))],
    )
    rims = [
        lax.ppermute(rim, "ctx", [(i, i + 1 + h) for i in range(GROUP - 1, devices - 1, GROUP)])
        for h, rim in enumerate(rims)
    ]
    message = trade(message, near)
    maps, own, lifted = call(
        chunk_kernel,
        [
            shape((ROW, 2 * HDIM, HDIM), BF16),
            shape((GROUP * SPAN, HDIM), F32),
            shape((GROUP * SPAN, HDIM), BF16),
        ],
        message,
        taps,
        *rims,
    )
    maps = trade(maps, rows)
    block = shape((HDIM, HDIM), BF16)
    step, add, mine = call(chain_kernel, [block, block, shape((HDIM, 2 * HDIM), F32)], maps)
    states = []
    for slab in range(SLAB - 1):
        leaving = call(relay_kernel, block, step, add, *states) if slab else add
        pairs = [(reach * slab + i, reach * (slab + 1) + i) for i in range(reach)]
        states.append(lax.ppermute(leaving, "ctx", pairs))
    normed = call(
        finish_kernel,
        shape((GROUP, SPAN, HDIM), BF16),
        *states,
        mine,
        own,
        lifted,
        norm_gain.reshape(1, -1),
    )
    normed = trade(normed, near)
    partial = call(project_kernel, shape((length, width), BF16), normed, output_gate, out_weight)
    partial = lax.all_to_all(partial.reshape(heads, length // heads, width), "head", 0, 0)
    return jnp.sum(partial.astype(F32), axis=0).astype(BF16)


def solution(mesh):
    in_specs = (
        P("ctx", "head"),
        P("ctx", "head"),
        P("ctx", "head"),
        P(None, None, "head"),
        P(None, "head"),
        P("ctx", "head"),
        P("ctx", "head"),
        P("ctx", "head"),
        P("head"),
        P(),
        P("head", None),
    )
    out_specs = P(("ctx", "head"), None)
    return jax.shard_map(local, mesh=mesh, in_specs=in_specs, out_specs=out_specs, check_vma=False)
```

```python
import jax
import jax.numpy as jnp
from jax import lax
from jax.experimental import pallas as pl
from jax.experimental.pallas import tpu as pltpu
from jax.sharding import PartitionSpec as P

HDIM = 128
CONV = 4
SPAN = 128
GROUP = 4
ROW = 4
SLAB = 4
EXTRA = 16
INTERPRET = False
F32 = jnp.float32
BF16 = jnp.bfloat16
NN = (((1,), (0,)), ((), ()))
NT = (((1,), (1,)), ((), ()))
TN = (((0,), (0,)), ((), ()))


def split2(a):
    high = a.astype(BF16)
    return high, (a - high.astype(F32)).astype(BF16)


def split3(a):
    high = a.astype(BF16)
    rest = a - high.astype(F32)
    mid = rest.astype(BF16)
    return high, mid, (rest - mid.astype(F32)).astype(BF16)


def dot1(a, b, dims=NN):
    return lax.dot_general(a.astype(BF16), b.astype(BF16), dims, preferred_element_type=F32)


def dot3(a, b, dims=NN):
    a_high, a_low = split2(a)
    b_high, b_low = split2(b)
    return dot1(a_high, b_high, dims) + (dot1(a_high, b_low, dims) + dot1(a_low, b_high, dims))


def dot_mixed(a, b, dims=NN):
    b_high, b_low = split2(b)
    return dot1(a, b_high, dims) + dot1(a, b_low, dims)


def softplus(x):
    y = jnp.exp(-jnp.abs(x))
    u = 1.0 + y
    log1p = jnp.where(u == 1.0, y, jnp.log(u) * (y / jnp.where(u == 1.0, 1.0, u - 1.0)))
    return jnp.maximum(x, 0.0) + log1p


def silu(v):
    return v / (1.0 + jnp.exp(-v))


def pack_kernel(
    q_hbm, k_hbm, v_hbm, qk_taps_hbm, v_taps_hbm, beta_hbm, gate_hbm, rate_ref, msg_ref, taps_ref,
    rim0, rim1, rim2, rim3, q_ref, k_ref, v_ref, qk_taps_ref, v_taps_ref, beta_ref, gate_ref, sems,
):
    rim_refs = (rim0, rim1, rim2, rim3)
    sources = (beta_hbm, gate_hbm, q_hbm, k_hbm, v_hbm, qk_taps_hbm, v_taps_hbm)
    targets = (beta_ref, gate_ref, q_ref, k_ref, v_ref, qk_taps_ref, v_taps_ref)
    copies = [pltpu.make_async_copy(x, y, sems.at[i]) for i, (x, y) in enumerate(zip(sources, targets))]
    for c in copies:
        c.start()
    length = q_ref.shape[0]
    ratio = v_ref.shape[1] // q_ref.shape[1]
    for c in copies[:2]:
        c.wait()
    beta = split3(jax.nn.sigmoid(beta_ref[...]))
    soft = softplus(gate_ref[...])
    head_row = lax.broadcasted_iota(jnp.int32, soft.shape, 0)
    rate = jnp.zeros(soft.shape, F32)
    for h in range(GROUP):
        rate = jnp.where(head_row == h, rate_ref[h], rate)
    decay = split3(-jnp.exp(rate) * soft)
    blank = jnp.zeros((EXTRA - 6, length), F32)
    for h in range(GROUP):
        rows = [p[h : h + 1].astype(F32) for p in beta + decay] + [blank]
        msg_ref[h, 3 * length :] = jnp.concatenate(rows, axis=0).astype(BF16)
    for c in copies[2:]:
        c.wait()
    for h in range(GROUP):
        kh = h // ratio
        query = q_ref[:, kh * HDIM : (kh + 1) * HDIM]
        keyed = k_ref[:, kh * HDIM : (kh + 1) * HDIM]
        value = v_ref[:, h * HDIM : (h + 1) * HDIM]
        msg_ref[h, 0:length] = query
        msg_ref[h, length : 2 * length] = keyed
        msg_ref[h, 2 * length : 3 * length] = value
        rim_refs[h][:, 0:HDIM] = query[length - 16 :]
        rim_refs[h][:, HDIM : 2 * HDIM] = keyed[length - 16 :]
        rim_refs[h][:, 2 * HDIM : 3 * HDIM] = value[length - 16 :]
    place = lax.axis_index("ctx") % GROUP

    def pick(taps, heads):
        parts = [taps[:, i * HDIM : (i + 1) * HDIM] for i in heads]
        got = parts[0]
        for i in range(1, GROUP):
            got = jnp.where(place == i, parts[i], got)
        return got

    key_heads = [h // ratio for h in range(GROUP)]
    taps_ref[0:4, :] = pick(qk_taps_ref[0].astype(F32), key_heads)
    taps_ref[4:8, :] = pick(qk_taps_ref[1].astype(F32), key_heads)
    taps_ref[8:12, :] = pick(v_taps_ref[...].astype(F32), range(GROUP))
    taps_ref[12:16, :] = jnp.zeros((4, HDIM), F32)


def chunk_kernel(msg_ref, taps_ref, rim0, rim1, rim2, rim3, map_ref, out_ref, lift_ref):
    length = SPAN
    total = GROUP * length
    rims = [r[8:16, :].astype(F32) for r in (rim0, rim1, rim2, rim3)]
    rim = (rims[0] + rims[1]) + (rims[2] + rims[3])

    def convolved(which):
        rows = [msg_ref[s, which * length : (which + 1) * length, :].astype(F32) for s in range(GROUP)]
        extended = jnp.concatenate([rim[:, which * HDIM : (which + 1) * HDIM]] + rows, axis=0)
        tap = taps_ref[4 * which : 4 * which + 4, :]
        acc = tap[CONV - 1 : CONV] * extended
        for by in range(1, CONV):
            acc = acc + tap[CONV - 1 - by : CONV - by] * pltpu.roll(extended, by, 0)
        return silu(acc[8 : 8 + total])

    query = convolved(0)
    query = query * (lax.rsqrt(jnp.sum(query * query, axis=-1, keepdims=True) + 1e-06) * HDIM ** (-0.5))
    keyed = convolved(1)
    keyed = keyed * lax.rsqrt(jnp.sum(keyed * keyed, axis=-1, keepdims=True) + 1e-06)
    value = convolved(2)

    row = lax.broadcasted_iota(jnp.int32, (length, length), 0)
    col = lax.broadcasted_iota(jnp.int32, (length, length), 1)
    eye = jnp.where(row == col, 1.0, 0.0)
    lower = jnp.where(row >= col, 1.0, 0.0).astype(BF16)
    eye_b = eye.astype(BF16)
    chunks = range(GROUP)
    at = lambda a, c: a[c * length : (c + 1) * length]
    extra = [msg_ref[s, 3 * length : 3 * length + EXTRA, :] for s in chunks]
    extra_f = [e.astype(F32) for e in extra]
    beta_row = [e[0:1] + e[1:2] + e[2:3] for e in extra_f]
    extra_col = [dot1(eye_b, e, NT) for e in extra]
    beta_col = [e[:, 0:1] + e[:, 1:2] + e[:, 2:3] for e in extra_col]
    run_row = [dot1(e, lower, NT) for e in extra]
    run_col = [dot1(lower, e, NT) for e in extra]
    gamma_row = [e[3:4] + e[4:5] + e[5:6] for e in run_row]
    gamma_col = [e[:, 3:4] + e[:, 4:5] + e[:, 5:6] for e in run_col]
    gamma_end = [g[length - 1 :] for g in gamma_col]
    within = [
        jnp.where(row >= col, jnp.exp(jnp.where(row >= col, jnp.minimum(gamma_col[c] - gamma_row[c], 0.0), 0.0)), 0.0)
        * beta_row[c]
        for c in chunks
    ]
    grow = [jnp.exp(g) for g in gamma_col]
    keys = [at(keyed, c) for c in chunks]
    queries = [at(query, c) for c in chunks]
    low = [jnp.where(row > col, within[c] * dot3(keys[c], keys[c], NT), 0.0) for c in chunks]
    inverse = [eye - jnp.where((row // 2) == (col // 2), low[c], 0.0) for c in chunks]
    size = 2
    while size < length:
        join = ((row // (2 * size)) == (col // (2 * size))) & ((row // size) > (col // size))
        step = [dot3(jnp.where(join, low[c], 0.0), inverse[c]) for c in chunks]
        inverse = [inverse[c] - dot3(inverse[c], step[c]) for c in chunks]
        size *= 2
    right = [jnp.concatenate([grow[c] * keys[c], at(value, c)], axis=1) for c in chunks]
    solved = [dot3(inverse[c], right[c]) for c in chunks]
    tail = [(jnp.exp(jnp.minimum(gamma_end[c] - gamma_col[c], 0.0)) * beta_col[c]) * keys[c] for c in chunks]
    pushed = [dot3(tail[c], solved[c], TN) for c in chunks]
    steps = [jnp.exp(gamma_end[c]) * eye - pushed[c][:, :HDIM] for c in chunks]
    adds = [pushed[c][:, HDIM:] for c in chunks]
    before = [None]
    state = jnp.concatenate([steps[0], adds[0]], axis=1)
    for c in range(1, GROUP):
        before.append(state)
        moved = dot3(steps[c], state)
        state = jnp.concatenate([moved[:, :HDIM], moved[:, HDIM:] + adds[c]], axis=1)
    for s in range(map_ref.shape[0]):
        map_ref[s, 0:HDIM, :] = state[:, :HDIM].astype(BF16)
        map_ref[s, HDIM : 2 * HDIM, :] = state[:, HDIM:].astype(BF16)
    scores = [within[c] * dot3(queries[c], keys[c], NT) for c in chunks]
    local = [dot3(scores[c], solved[c]) for c in chunks]
    for c in chunks:
        lifted = grow[c] * queries[c] - local[c][:, :HDIM]
        own = local[c][:, HDIM:]
        if c:
            both = dot3(lifted, before[c])
            lifted = both[:, :HDIM]
            own = own + both[:, HDIM:]
        out_ref[c * length : (c + 1) * length, :] = own
        lift_ref[c * length : (c + 1) * length, :] = lifted.astype(BF16)


def chain_kernel(maps_ref, step_ref, add_ref, mine_ref):
    place = (lax.axis_index("ctx") // GROUP) % ROW
    row = lax.broadcasted_iota(jnp.int32, (HDIM, 2 * HDIM), 0)
    col = lax.broadcasted_iota(jnp.int32, (HDIM, 2 * HDIM), 1)
    mine = jnp.where(row == col, 1.0, 0.0)
    state = jnp.concatenate([maps_ref[0, :HDIM, :], maps_ref[0, HDIM:, :]], axis=1).astype(F32)
    for i in range(1, ROW):
        mine = jnp.where(place == i, state, mine)
        moved = dot_mixed(maps_ref[i, :HDIM, :], state)
        state = jnp.concatenate(
            [moved[:, :HDIM], moved[:, HDIM:] + maps_ref[i, HDIM:, :].astype(F32)], axis=1
        )
    step_ref[...] = state[:, :HDIM].astype(BF16)
    add_ref[...] = state[:, HDIM:].astype(BF16)
    mine_ref[...] = mine


def relay_kernel(step_ref, add_ref, *refs):
    state = refs[0][...]
    for r in refs[1:-1]:
        state = state + r[...]
    refs[-1][...] = (dot1(step_ref[...], state) + add_ref[...].astype(F32)).astype(BF16)


def finish_kernel(first_ref, second_ref, third_ref, mine_ref, own_ref, lift_ref, gain_ref, normed_ref):
    got = first_ref[...].astype(F32) + second_ref[...].astype(F32) + third_ref[...].astype(F32)
    start = dot3(mine_ref[:, :HDIM], got) + mine_ref[:, HDIM:]
    core = own_ref[...] + dot_mixed(lift_ref[...], start)
    mean = jnp.mean(core * core, axis=-1, keepdims=True)
    normed = (core * lax.rsqrt(mean + 1e-06) * gain_ref[...]).astype(BF16)
    for s in range(GROUP):
        normed_ref[s] = normed[s * SPAN : (s + 1) * SPAN]


def project_kernel(normed_ref, gate_ref, weight_ref, partial_ref):
    parts = []
    for h in range(GROUP):
        gate = silu(gate_ref[:, h * HDIM : (h + 1) * HDIM].astype(F32))
        parts.append((normed_ref[h].astype(F32) * gate).astype(BF16))
    left = jnp.concatenate(parts, axis=1)
    partial_ref[...] = lax.dot_general(
        left, weight_ref[...], NN, preferred_element_type=F32
    ).astype(BF16)


def call(body, outs, *args, **more):
    return pl.pallas_call(
        body,
        out_shape=outs,
        compiler_params=pltpu.CompilerParams(vmem_limit_bytes=32 * 1024 * 1024),
        interpret=pltpu.InterpretParams() if INTERPRET else False,
        **more,
    )(*args)


def in_hbm(a):
    return a if INTERPRET else pltpu.with_memory_space_constraint(a, pltpu.HBM)


def local(
    query_raw,
    key_raw,
    value_raw,
    query_key_conv,
    value_conv,
    output_gate,
    beta_logit,
    gate_logit,
    log_rate,
    norm_gain,
    out_weight,
):
    shape = jax.ShapeDtypeStruct
    devices = lax.axis_size("ctx")
    heads = lax.axis_size("head")
    length = query_raw.shape[0]
    width = out_weight.shape[1]
    near = [[GROUP * g + i for i in range(GROUP)] for g in range(devices // GROUP)]
    reach = GROUP * ROW
    rows = [
        [z * reach + GROUP * r + i for r in range(ROW)]
        for z in range(devices // reach)
        for i in range(GROUP)
    ]

    def trade(a, groups):
        return lax.all_to_all(a, "ctx", 0, 0, axis_index_groups=groups)

    raw = (query_raw, key_raw, value_raw, query_key_conv, value_conv, beta_logit.T, gate_logit.T)
    fetched = [pltpu.VMEM(raw[i].shape, raw[i].dtype) for i in range(len(raw))]
    message, taps, *rims = call(
        pack_kernel,
        [shape((GROUP, 3 * length + EXTRA, HDIM), BF16), shape((16, HDIM), F32)]
        + [shape((16, 3 * HDIM), BF16)] * GROUP,
        *[in_hbm(a) for a in raw],
        in_hbm(log_rate),
        in_specs=[pl.BlockSpec(memory_space=pltpu.HBM)] * len(raw) + [pl.BlockSpec(memory_space=pltpu.SMEM)],
        scratch_shapes=fetched + [pltpu.SemaphoreType.DMA((len(raw),))],
    )
    rims = [
        lax.ppermute(rim, "ctx", [(i, i + 1 + h) for i in range(GROUP - 1, devices - 1, GROUP)])
        for h, rim in enumerate(rims)
    ]
    message = trade(message, near)
    message, out_weight, output_gate = lax.optimization_barrier((message, out_weight, output_gate))
    maps, own, lifted = call(
        chunk_kernel,
        [
            shape((ROW, 2 * HDIM, HDIM), BF16),
            shape((GROUP * SPAN, HDIM), F32),
            shape((GROUP * SPAN, HDIM), BF16),
        ],
        message,
        taps,
        *rims,
    )
    maps = trade(maps, rows)
    block = shape((HDIM, HDIM), BF16)
    step, add, mine = call(chain_kernel, [block, block, shape((HDIM, 2 * HDIM), F32)], maps)
    states = []
    for slab in range(SLAB - 1):
        leaving = call(relay_kernel, block, step, add, *states) if slab else add
        pairs = [(reach * slab + i, reach * (slab + 1) + i) for i in range(reach)]
        states.append(lax.ppermute(leaving, "ctx", pairs))
    normed = call(
        finish_kernel,
        shape((GROUP, SPAN, HDIM), BF16),
        *states,
        mine,
        own,
        lifted,
        norm_gain.reshape(1, -1),
    )
    normed = trade(normed, near)
    partial = call(project_kernel, shape((length, width), BF16), normed, output_gate, out_weight)
    partial = lax.all_to_all(partial.reshape(heads, length // heads, width), "head", 0, 0)
    return jnp.sum(partial.astype(F32), axis=0).astype(BF16)


def solution(mesh):
    in_specs = (
        P("ctx", "head"),
        P("ctx", "head"),
        P("ctx", "head"),
        P(None, None, "head"),
        P(None, "head"),
        P("ctx", "head"),
        P("ctx", "head"),
        P("ctx", "head"),
        P("head"),
        P(),
        P("head", None),
    )
    out_specs = P(("ctx", "head"), None)
    return jax.shard_map(local, mesh=mesh, in_specs=in_specs, out_specs=out_specs, check_vma=False)
```

```python
import jax
import jax.numpy as jnp
from jax import lax
from jax.experimental import pallas as pl
from jax.experimental.pallas import tpu as pltpu
from jax.sharding import PartitionSpec as P

HDIM = 128
CONV = 4
SPAN = 128
GROUP = 4
ROW = 4
SLAB = 4
EXTRA = 16
INTERPRET = False
F32 = jnp.float32
BF16 = jnp.bfloat16
NN = (((1,), (0,)), ((), ()))
NT = (((1,), (1,)), ((), ()))
TN = (((0,), (0,)), ((), ()))


def split2(a):
    high = a.astype(BF16)
    return high, (a - high.astype(F32)).astype(BF16)


def split3(a):
    high = a.astype(BF16)
    rest = a - high.astype(F32)
    mid = rest.astype(BF16)
    return high, mid, (rest - mid.astype(F32)).astype(BF16)


def dot1(a, b, dims=NN):
    return lax.dot_general(a.astype(BF16), b.astype(BF16), dims, preferred_element_type=F32)


def dot3(a, b, dims=NN):
    a_high, a_low = split2(a)
    b_high, b_low = split2(b)
    return dot1(a_high, b_high, dims) + (dot1(a_high, b_low, dims) + dot1(a_low, b_high, dims))


def dot_mixed(a, b, dims=NN):
    b_high, b_low = split2(b)
    return dot1(a, b_high, dims) + dot1(a, b_low, dims)


def softplus(x):
    y = jnp.exp(-jnp.abs(x))
    u = 1.0 + y
    log1p = jnp.where(u == 1.0, y, jnp.log(u) * (y / jnp.where(u == 1.0, 1.0, u - 1.0)))
    return jnp.maximum(x, 0.0) + log1p


def silu(v):
    return v / (1.0 + jnp.exp(-v))


def pack_kernel(
    q_hbm, k_hbm, v_hbm, qk_taps_hbm, v_taps_hbm, beta_hbm, gate_hbm, rate_ref, msg_ref, taps_ref,
    rim0, rim1, rim2, rim3, q_ref, k_ref, v_ref, qk_taps_ref, v_taps_ref, beta_ref, gate_ref, sems,
):
    rim_refs = (rim0, rim1, rim2, rim3)
    sources = (beta_hbm, gate_hbm, q_hbm, k_hbm, v_hbm, qk_taps_hbm, v_taps_hbm)
    targets = (beta_ref, gate_ref, q_ref, k_ref, v_ref, qk_taps_ref, v_taps_ref)
    copies = [pltpu.make_async_copy(x, y, sems.at[i]) for i, (x, y) in enumerate(zip(sources, targets))]
    for c in copies:
        c.start()
    length = q_ref.shape[0]
    ratio = v_ref.shape[1] // q_ref.shape[1]
    for c in copies[:2]:
        c.wait()
    beta = split3(jax.nn.sigmoid(beta_ref[...]))
    soft = softplus(gate_ref[...])
    head_row = lax.broadcasted_iota(jnp.int32, soft.shape, 0)
    rate = jnp.zeros(soft.shape, F32)
    for h in range(GROUP):
        rate = jnp.where(head_row == h, rate_ref[h], rate)
    decay = split3(-jnp.exp(rate) * soft)
    blank = jnp.zeros((EXTRA - 6, length), F32)
    for h in range(GROUP):
        rows = [p[h : h + 1].astype(F32) for p in beta + decay] + [blank]
        msg_ref[h, 3 * length :] = jnp.concatenate(rows, axis=0).astype(BF16)
    for c in copies[2:]:
        c.wait()
    for h in range(GROUP):
        kh = h // ratio
        query = q_ref[:, kh * HDIM : (kh + 1) * HDIM]
        keyed = k_ref[:, kh * HDIM : (kh + 1) * HDIM]
        value = v_ref[:, h * HDIM : (h + 1) * HDIM]
        msg_ref[h, 0:length] = query
        msg_ref[h, length : 2 * length] = keyed
        msg_ref[h, 2 * length : 3 * length] = value
        rim_refs[h][:, 0:HDIM] = query[length - 16 :]
        rim_refs[h][:, HDIM : 2 * HDIM] = keyed[length - 16 :]
        rim_refs[h][:, 2 * HDIM : 3 * HDIM] = value[length - 16 :]
    place = lax.axis_index("ctx") % GROUP

    def pick(taps, heads):
        parts = [taps[:, i * HDIM : (i + 1) * HDIM] for i in heads]
        got = parts[0]
        for i in range(1, GROUP):
            got = jnp.where(place == i, parts[i], got)
        return got

    key_heads = [h // ratio for h in range(GROUP)]
    taps_ref[0:4, :] = pick(qk_taps_ref[0].astype(F32), key_heads)
    taps_ref[4:8, :] = pick(qk_taps_ref[1].astype(F32), key_heads)
    taps_ref[8:12, :] = pick(v_taps_ref[...].astype(F32), range(GROUP))
    taps_ref[12:16, :] = jnp.zeros((4, HDIM), F32)


def chunk_kernel(msg_ref, taps_ref, rim0, rim1, rim2, rim3, map_ref, out_ref, lift_ref):
    length = SPAN
    total = GROUP * length
    rims = [r[8:16, :].astype(F32) for r in (rim0, rim1, rim2, rim3)]
    rim = (rims[0] + rims[1]) + (rims[2] + rims[3])

    def convolved(which):
        rows = [msg_ref[s, which * length : (which + 1) * length, :].astype(F32) for s in range(GROUP)]
        extended = jnp.concatenate([rim[:, which * HDIM : (which + 1) * HDIM]] + rows, axis=0)
        tap = taps_ref[4 * which : 4 * which + 4, :]
        acc = tap[CONV - 1 : CONV] * extended
        for by in range(1, CONV):
            acc = acc + tap[CONV - 1 - by : CONV - by] * pltpu.roll(extended, by, 0)
        return silu(acc[8 : 8 + total])

    query = convolved(0)
    query = query * (lax.rsqrt(jnp.sum(query * query, axis=-1, keepdims=True) + 1e-06) * HDIM ** (-0.5))
    keyed = convolved(1)
    keyed = keyed * lax.rsqrt(jnp.sum(keyed * keyed, axis=-1, keepdims=True) + 1e-06)
    value = convolved(2)

    row = lax.broadcasted_iota(jnp.int32, (length, length), 0)
    col = lax.broadcasted_iota(jnp.int32, (length, length), 1)
    eye = jnp.where(row == col, 1.0, 0.0)
    lower = jnp.where(row >= col, 1.0, 0.0).astype(BF16)
    eye_b = eye.astype(BF16)
    chunks = range(GROUP)
    at = lambda a, c: a[c * length : (c + 1) * length]
    extra = [msg_ref[s, 3 * length : 3 * length + EXTRA, :] for s in chunks]
    extra_f = [e.astype(F32) for e in extra]
    beta_row = [e[0:1] + e[1:2] + e[2:3] for e in extra_f]
    extra_col = [dot1(eye_b, e, NT) for e in extra]
    beta_col = [e[:, 0:1] + e[:, 1:2] + e[:, 2:3] for e in extra_col]
    run_row = [dot1(e, lower, NT) for e in extra]
    run_col = [dot1(lower, e, NT) for e in extra]
    gamma_row = [e[3:4] + e[4:5] + e[5:6] for e in run_row]
    gamma_col = [e[:, 3:4] + e[:, 4:5] + e[:, 5:6] for e in run_col]
    gamma_end = [g[length - 1 :] for g in gamma_col]
    within = [
        jnp.where(row >= col, jnp.exp(jnp.where(row >= col, jnp.minimum(gamma_col[c] - gamma_row[c], 0.0), 0.0)), 0.0)
        * beta_row[c]
        for c in chunks
    ]
    grow = [jnp.exp(g) for g in gamma_col]
    keys = [at(keyed, c) for c in chunks]
    queries = [at(query, c) for c in chunks]
    low = [jnp.where(row > col, within[c] * dot3(keys[c], keys[c], NT), 0.0) for c in chunks]
    inverse = [eye - jnp.where((row // 2) == (col // 2), low[c], 0.0) for c in chunks]
    size = 2
    while size < length:
        join = ((row // (2 * size)) == (col // (2 * size))) & ((row // size) > (col // size))
        step = [dot3(jnp.where(join, low[c], 0.0), inverse[c]) for c in chunks]
        inverse = [inverse[c] - dot3(inverse[c], step[c]) for c in chunks]
        size *= 2
    right = [jnp.concatenate([grow[c] * keys[c], at(value, c)], axis=1) for c in chunks]
    solved = [dot3(inverse[c], right[c]) for c in chunks]
    tail = [(jnp.exp(jnp.minimum(gamma_end[c] - gamma_col[c], 0.0)) * beta_col[c]) * keys[c] for c in chunks]
    pushed = [dot3(tail[c], solved[c], TN) for c in chunks]
    steps = [jnp.exp(gamma_end[c]) * eye - pushed[c][:, :HDIM] for c in chunks]
    adds = [pushed[c][:, HDIM:] for c in chunks]
    before = [None]
    state = jnp.concatenate([steps[0], adds[0]], axis=1)
    for c in range(1, GROUP):
        before.append(state)
        moved = dot3(steps[c], state)
        state = jnp.concatenate([moved[:, :HDIM], moved[:, HDIM:] + adds[c]], axis=1)
    for s in range(map_ref.shape[0]):
        map_ref[s, 0:HDIM, :] = state[:, :HDIM].astype(BF16)
        map_ref[s, HDIM : 2 * HDIM, :] = state[:, HDIM:].astype(BF16)
    scores = [within[c] * dot3(queries[c], keys[c], NT) for c in chunks]
    local = [dot3(scores[c], solved[c]) for c in chunks]
    for c in chunks:
        lifted = grow[c] * queries[c] - local[c][:, :HDIM]
        own = local[c][:, HDIM:]
        if c:
            both = dot3(lifted, before[c])
            lifted = both[:, :HDIM]
            own = own + both[:, HDIM:]
        out_ref[c * length : (c + 1) * length, :] = own
        lift_ref[c * length : (c + 1) * length, :] = lifted.astype(BF16)


def chain_kernel(maps_ref, step_ref, add_ref, mine_ref):
    place = (lax.axis_index("ctx") // GROUP) % ROW
    row = lax.broadcasted_iota(jnp.int32, (HDIM, 2 * HDIM), 0)
    col = lax.broadcasted_iota(jnp.int32, (HDIM, 2 * HDIM), 1)
    mine = jnp.where(row == col, 1.0, 0.0)
    state = jnp.concatenate([maps_ref[0, :HDIM, :], maps_ref[0, HDIM:, :]], axis=1).astype(F32)
    for i in range(1, ROW):
        mine = jnp.where(place == i, state, mine)
        moved = dot_mixed(maps_ref[i, :HDIM, :], state)
        state = jnp.concatenate(
            [moved[:, :HDIM], moved[:, HDIM:] + maps_ref[i, HDIM:, :].astype(F32)], axis=1
        )
    step_ref[...] = state[:, :HDIM].astype(BF16)
    add_ref[...] = state[:, HDIM:].astype(BF16)
    mine_ref[...] = mine


def relay_kernel(step_ref, add_ref, *refs):
    state = refs[0][...]
    for r in refs[1:-1]:
        state = state + r[...]
    refs[-1][...] = (dot1(step_ref[...], state) + add_ref[...].astype(F32)).astype(BF16)


def finish_kernel(first_ref, second_ref, third_ref, mine_ref, own_ref, lift_ref, gain_ref, normed_ref):
    got = first_ref[...].astype(F32) + second_ref[...].astype(F32) + third_ref[...].astype(F32)
    high, low = split2(mine_ref[:, :HDIM])
    start = dot1(high, got) + dot1(low, got) + mine_ref[:, HDIM:]
    core = own_ref[...] + dot_mixed(lift_ref[...], start)
    mean = jnp.mean(core * core, axis=-1, keepdims=True)
    normed = (core * lax.rsqrt(mean + 1e-06) * gain_ref[...]).astype(BF16)
    for s in range(GROUP):
        normed_ref[s] = normed[s * SPAN : (s + 1) * SPAN]


def project_kernel(normed_ref, gate_ref, weight_ref, partial_ref):
    parts = []
    for h in range(GROUP):
        gate = silu(gate_ref[:, h * HDIM : (h + 1) * HDIM].astype(F32))
        parts.append((normed_ref[h].astype(F32) * gate).astype(BF16))
    left = jnp.concatenate(parts, axis=1)
    partial_ref[...] = lax.dot_general(
        left, weight_ref[...], NN, preferred_element_type=F32
    ).astype(BF16)


def call(body, outs, *args, **more):
    return pl.pallas_call(
        body,
        out_shape=outs,
        compiler_params=pltpu.CompilerParams(vmem_limit_bytes=32 * 1024 * 1024),
        interpret=pltpu.InterpretParams() if INTERPRET else False,
        **more,
    )(*args)


def in_hbm(a):
    return a if INTERPRET else pltpu.with_memory_space_constraint(a, pltpu.HBM)


def local(
    query_raw,
    key_raw,
    value_raw,
    query_key_conv,
    value_conv,
    output_gate,
    beta_logit,
    gate_logit,
    log_rate,
    norm_gain,
    out_weight,
):
    shape = jax.ShapeDtypeStruct
    devices = lax.axis_size("ctx")
    heads = lax.axis_size("head")
    length = query_raw.shape[0]
    width = out_weight.shape[1]
    near = [[GROUP * g + i for i in range(GROUP)] for g in range(devices // GROUP)]
    reach = GROUP * ROW
    rows = [
        [z * reach + GROUP * r + i for r in range(ROW)]
        for z in range(devices // reach)
        for i in range(GROUP)
    ]

    def trade(a, groups):
        return lax.all_to_all(a, "ctx", 0, 0, axis_index_groups=groups)

    raw = (query_raw, key_raw, value_raw, query_key_conv, value_conv, beta_logit.T, gate_logit.T)
    fetched = [pltpu.VMEM(raw[i].shape, raw[i].dtype) for i in range(len(raw))]
    message, taps, *rims = call(
        pack_kernel,
        [shape((GROUP, 3 * length + EXTRA, HDIM), BF16), shape((16, HDIM), F32)]
        + [shape((16, 3 * HDIM), BF16)] * GROUP,
        *[in_hbm(a) for a in raw],
        in_hbm(log_rate),
        in_specs=[pl.BlockSpec(memory_space=pltpu.HBM)] * len(raw) + [pl.BlockSpec(memory_space=pltpu.SMEM)],
        scratch_shapes=fetched + [pltpu.SemaphoreType.DMA((len(raw),))],
    )
    rims = [
        lax.ppermute(rim, "ctx", [(i, i + 1 + h) for i in range(GROUP - 1, devices - 1, GROUP)])
        for h, rim in enumerate(rims)
    ]
    message = trade(message, near)
    message, out_weight, output_gate = lax.optimization_barrier((message, out_weight, output_gate))
    maps, own, lifted = call(
        chunk_kernel,
        [
            shape((ROW, 2 * HDIM, HDIM), BF16),
            shape((GROUP * SPAN, HDIM), F32),
            shape((GROUP * SPAN, HDIM), BF16),
        ],
        message,
        taps,
        *rims,
    )
    maps = trade(maps, rows)
    block = shape((HDIM, HDIM), BF16)
    step, add, mine = call(chain_kernel, [block, block, shape((HDIM, 2 * HDIM), F32)], maps)
    states = []
    for slab in range(SLAB - 1):
        leaving = call(relay_kernel, block, step, add, *states) if slab else add
        pairs = [(reach * slab + i, reach * (slab + 1) + i) for i in range(reach)]
        states.append(lax.ppermute(leaving, "ctx", pairs))
    normed = call(
        finish_kernel,
        shape((GROUP, SPAN, HDIM), BF16),
        *states,
        mine,
        own,
        lifted,
        norm_gain.reshape(1, -1),
    )
    normed = trade(normed, near)
    partial = call(project_kernel, shape((length, width), BF16), normed, output_gate, out_weight)
    partial = lax.all_to_all(partial.reshape(heads, length // heads, width), "head", 0, 0)
    return jnp.sum(partial.astype(F32), axis=0).astype(BF16)


def solution(mesh):
    in_specs = (
        P("ctx", "head"),
        P("ctx", "head"),
        P("ctx", "head"),
        P(None, None, "head"),
        P(None, "head"),
        P("ctx", "head"),
        P("ctx", "head"),
        P("ctx", "head"),
        P("head"),
        P(),
        P("head", None),
    )
    out_specs = P(("ctx", "head"), None)
    return jax.shard_map(local, mesh=mesh, in_specs=in_specs, out_specs=out_specs, check_vma=False)
```

```python
import jax
import jax.numpy as jnp
from jax import lax
from jax.experimental import pallas as pl
from jax.experimental.pallas import tpu as pltpu
from jax.sharding import PartitionSpec as P

HDIM = 128
CONV = 4
SPAN = 128
GROUP = 4
ROW = 4
SLAB = 4
EXTRA = 16
INTERPRET = False
F32 = jnp.float32
BF16 = jnp.bfloat16
NN = (((1,), (0,)), ((), ()))
NT = (((1,), (1,)), ((), ()))
TN = (((0,), (0,)), ((), ()))


def split2(a):
    high = a.astype(BF16)
    return high, (a - high.astype(F32)).astype(BF16)


def split3(a):
    high = a.astype(BF16)
    rest = a - high.astype(F32)
    mid = rest.astype(BF16)
    return high, mid, (rest - mid.astype(F32)).astype(BF16)


def dot1(a, b, dims=NN):
    return lax.dot_general(a.astype(BF16), b.astype(BF16), dims, preferred_element_type=F32)


def dot3(a, b, dims=NN):
    a_high, a_low = split2(a)
    b_high, b_low = split2(b)
    return dot1(a_high, b_high, dims) + (dot1(a_high, b_low, dims) + dot1(a_low, b_high, dims))


def dot_mixed(a, b, dims=NN):
    b_high, b_low = split2(b)
    return dot1(a, b_high, dims) + dot1(a, b_low, dims)


def softplus(x):
    y = jnp.exp(-jnp.abs(x))
    u = 1.0 + y
    log1p = jnp.where(u == 1.0, y, jnp.log(u) * (y / jnp.where(u == 1.0, 1.0, u - 1.0)))
    return jnp.maximum(x, 0.0) + log1p


def silu(v):
    return v / (1.0 + jnp.exp(-v))


def pack_kernel(
    q_hbm, k_hbm, v_hbm, qk_taps_hbm, v_taps_hbm, beta_hbm, gate_hbm, rate_ref, msg_ref, taps_ref,
    rim0, rim1, rim2, rim3, q_ref, k_ref, v_ref, qk_taps_ref, v_taps_ref, beta_ref, gate_ref, sems,
):
    rim_refs = (rim0, rim1, rim2, rim3)
    sources = (beta_hbm, gate_hbm, q_hbm, k_hbm, v_hbm, qk_taps_hbm, v_taps_hbm)
    targets = (beta_ref, gate_ref, q_ref, k_ref, v_ref, qk_taps_ref, v_taps_ref)
    copies = [pltpu.make_async_copy(x, y, sems.at[i]) for i, (x, y) in enumerate(zip(sources, targets))]
    for c in copies:
        c.start()
    length = q_ref.shape[0]
    ratio = v_ref.shape[1] // q_ref.shape[1]
    for c in copies[:2]:
        c.wait()
    beta = split3(jax.nn.sigmoid(beta_ref[...]))
    soft = softplus(gate_ref[...])
    head_row = lax.broadcasted_iota(jnp.int32, soft.shape, 0)
    rate = jnp.zeros(soft.shape, F32)
    for h in range(GROUP):
        rate = jnp.where(head_row == h, rate_ref[h], rate)
    decay = split3(-jnp.exp(rate) * soft)
    blank = jnp.zeros((EXTRA - 6, length), F32)
    for h in range(GROUP):
        rows = [p[h : h + 1].astype(F32) for p in beta + decay] + [blank]
        msg_ref[h, 3 * length :] = jnp.concatenate(rows, axis=0).astype(BF16)
    for c in copies[2:]:
        c.wait()
    for h in range(GROUP):
        kh = h // ratio
        query = q_ref[:, kh * HDIM : (kh + 1) * HDIM]
        keyed = k_ref[:, kh * HDIM : (kh + 1) * HDIM]
        value = v_ref[:, h * HDIM : (h + 1) * HDIM]
        msg_ref[h, 0:length] = query
        msg_ref[h, length : 2 * length] = keyed
        msg_ref[h, 2 * length : 3 * length] = value
        rim_refs[h][:, 0:HDIM] = query[length - 16 :]
        rim_refs[h][:, HDIM : 2 * HDIM] = keyed[length - 16 :]
        rim_refs[h][:, 2 * HDIM : 3 * HDIM] = value[length - 16 :]
    place = lax.axis_index("ctx") % GROUP

    def pick(taps, heads):
        parts = [taps[:, i * HDIM : (i + 1) * HDIM] for i in heads]
        got = parts[0]
        for i in range(1, GROUP):
            got = jnp.where(place == i, parts[i], got)
        return got

    key_heads = [h // ratio for h in range(GROUP)]
    taps_ref[0:4, :] = pick(qk_taps_ref[0].astype(F32), key_heads)
    taps_ref[4:8, :] = pick(qk_taps_ref[1].astype(F32), key_heads)
    taps_ref[8:12, :] = pick(v_taps_ref[...].astype(F32), range(GROUP))
    taps_ref[12:16, :] = jnp.zeros((4, HDIM), F32)


def chunk_kernel(msg_ref, taps_ref, rim0, rim1, rim2, rim3, map_ref, out_ref, lift_ref):
    length = SPAN
    total = GROUP * length
    rims = [r[8:16, :].astype(F32) for r in (rim0, rim1, rim2, rim3)]
    rim = (rims[0] + rims[1]) + (rims[2] + rims[3])

    def convolved(which):
        rows = [msg_ref[s, which * length : (which + 1) * length, :].astype(F32) for s in range(GROUP)]
        extended = jnp.concatenate([rim[:, which * HDIM : (which + 1) * HDIM]] + rows, axis=0)
        tap = taps_ref[4 * which : 4 * which + 4, :]
        acc = tap[CONV - 1 : CONV] * extended
        for by in range(1, CONV):
            acc = acc + tap[CONV - 1 - by : CONV - by] * pltpu.roll(extended, by, 0)
        return silu(acc[8 : 8 + total])

    query = convolved(0)
    query = query * (lax.rsqrt(jnp.sum(query * query, axis=-1, keepdims=True) + 1e-06) * HDIM ** (-0.5))
    keyed = convolved(1)
    keyed = keyed * lax.rsqrt(jnp.sum(keyed * keyed, axis=-1, keepdims=True) + 1e-06)
    value = convolved(2)

    row = lax.broadcasted_iota(jnp.int32, (length, length), 0)
    col = lax.broadcasted_iota(jnp.int32, (length, length), 1)
    eye = jnp.where(row == col, 1.0, 0.0)
    lower = jnp.where(row >= col, 1.0, 0.0).astype(BF16)
    eye_b = eye.astype(BF16)
    chunks = range(GROUP)
    at = lambda a, c: a[c * length : (c + 1) * length]
    extra = [msg_ref[s, 3 * length : 3 * length + EXTRA, :] for s in chunks]
    extra_f = [e.astype(F32) for e in extra]
    beta_row = [e[0:1] + e[1:2] + e[2:3] for e in extra_f]
    extra_col = [dot1(eye_b, e, NT) for e in extra]
    beta_col = [e[:, 0:1] + e[:, 1:2] + e[:, 2:3] for e in extra_col]
    run_row = [dot1(e, lower, NT) for e in extra]
    run_col = [dot1(lower, e, NT) for e in extra]
    gamma_row = [e[3:4] + e[4:5] + e[5:6] for e in run_row]
    gamma_col = [e[:, 3:4] + e[:, 4:5] + e[:, 5:6] for e in run_col]
    gamma_end = [g[length - 1 :] for g in gamma_col]
    within = [
        jnp.where(row >= col, jnp.exp(jnp.where(row >= col, jnp.minimum(gamma_col[c] - gamma_row[c], 0.0), 0.0)), 0.0)
        * beta_row[c]
        for c in chunks
    ]
    grow = [jnp.exp(g) for g in gamma_col]
    keys = [at(keyed, c) for c in chunks]
    queries = [at(query, c) for c in chunks]
    low = [jnp.where(row > col, within[c] * dot3(keys[c], keys[c], NT), 0.0) for c in chunks]
    inverse = [eye - jnp.where((row // 2) == (col // 2), low[c], 0.0) for c in chunks]
    size = 2
    while size < length:
        join = ((row // (2 * size)) == (col // (2 * size))) & ((row // size) > (col // size))
        step = [dot3(jnp.where(join, low[c], 0.0), inverse[c]) for c in chunks]
        inverse = [inverse[c] - dot3(inverse[c], step[c]) for c in chunks]
        size *= 2
    right = [jnp.concatenate([grow[c] * keys[c], at(value, c)], axis=1) for c in chunks]
    solved = [dot3(inverse[c], right[c]) for c in chunks]
    tail = [(jnp.exp(jnp.minimum(gamma_end[c] - gamma_col[c], 0.0)) * beta_col[c]) * keys[c] for c in chunks]
    pushed = [dot3(tail[c], solved[c], TN) for c in chunks]
    steps = [jnp.exp(gamma_end[c]) * eye - pushed[c][:, :HDIM] for c in chunks]
    adds = [pushed[c][:, HDIM:] for c in chunks]
    before = [None]
    state = jnp.concatenate([steps[0], adds[0]], axis=1)
    for c in range(1, GROUP):
        before.append(state)
        moved = dot3(steps[c], state)
        state = jnp.concatenate([moved[:, :HDIM], moved[:, HDIM:] + adds[c]], axis=1)
    for s in range(map_ref.shape[0]):
        map_ref[s, 0:HDIM, :] = state[:, :HDIM].astype(BF16)
        map_ref[s, HDIM : 2 * HDIM, :] = state[:, HDIM:].astype(BF16)
    scores = [within[c] * dot3(queries[c], keys[c], NT) for c in chunks]
    local = [dot3(scores[c], solved[c]) for c in chunks]
    for c in chunks:
        lifted = grow[c] * queries[c] - local[c][:, :HDIM]
        own = local[c][:, HDIM:]
        if c:
            both = dot3(lifted, before[c])
            lifted = both[:, :HDIM]
            own = own + both[:, HDIM:]
        out_ref[c * length : (c + 1) * length, :] = own
        lift_ref[c * length : (c + 1) * length, :] = lifted.astype(BF16)


def chain_kernel(maps_ref, step_ref, add_ref, mine_ref):
    place = (lax.axis_index("ctx") // GROUP) % ROW
    row = lax.broadcasted_iota(jnp.int32, (HDIM, 2 * HDIM), 0)
    col = lax.broadcasted_iota(jnp.int32, (HDIM, 2 * HDIM), 1)
    mine = jnp.where(row == col, 1.0, 0.0)
    state = jnp.concatenate([maps_ref[0, :HDIM, :], maps_ref[0, HDIM:, :]], axis=1).astype(F32)
    for i in range(1, ROW):
        mine = jnp.where(place == i, state, mine)
        moved = dot_mixed(maps_ref[i, :HDIM, :], state)
        state = jnp.concatenate(
            [moved[:, :HDIM], moved[:, HDIM:] + maps_ref[i, HDIM:, :].astype(F32)], axis=1
        )
    step_ref[...] = state[:, :HDIM].astype(BF16)
    add_ref[...] = state[:, HDIM:].astype(BF16)
    mine_ref[...] = mine


def relay_kernel(step_ref, add_ref, *refs):
    state = refs[0][...]
    for r in refs[1:-1]:
        state = state + r[...]
    refs[-1][...] = (dot1(step_ref[...], state) + add_ref[...].astype(F32)).astype(BF16)


def finish_kernel(first_ref, second_ref, third_ref, mine_ref, own_ref, lift_ref, gain_ref, normed_ref):
    got = first_ref[...].astype(F32) + second_ref[...].astype(F32) + third_ref[...].astype(F32)
    start = dot3(mine_ref[:, :HDIM], got) + mine_ref[:, HDIM:]
    core = own_ref[...] + dot_mixed(lift_ref[...], start)
    mean = jnp.mean(core * core, axis=-1, keepdims=True)
    normed = (core * lax.rsqrt(mean + 1e-06) * gain_ref[...]).astype(BF16)
    for s in range(GROUP):
        normed_ref[s] = normed[s * SPAN : (s + 1) * SPAN]


def project_kernel(normed_ref, gate_ref, weight_ref, partial_ref):
    parts = []
    for h in range(GROUP):
        gate = silu(gate_ref[:, h * HDIM : (h + 1) * HDIM].astype(F32))
        parts.append((normed_ref[h].astype(F32) * gate).astype(BF16))
    left = jnp.concatenate(parts, axis=1)
    partial_ref[...] = lax.dot_general(
        left, weight_ref[...], NN, preferred_element_type=F32
    ).astype(BF16)


def sum_kernel(parts_ref, out_ref):
    total = parts_ref[0].astype(F32)
    for i in range(1, parts_ref.shape[0]):
        total = total + parts_ref[i].astype(F32)
    out_ref[...] = total.astype(BF16)


def call(body, outs, *args, **more):
    return pl.pallas_call(
        body,
        out_shape=outs,
        compiler_params=pltpu.CompilerParams(vmem_limit_bytes=32 * 1024 * 1024),
        interpret=pltpu.InterpretParams() if INTERPRET else False,
        **more,
    )(*args)


def in_hbm(a):
    return a if INTERPRET else pltpu.with_memory_space_constraint(a, pltpu.HBM)


def local(
    query_raw,
    key_raw,
    value_raw,
    query_key_conv,
    value_conv,
    output_gate,
    beta_logit,
    gate_logit,
    log_rate,
    norm_gain,
    out_weight,
):
    shape = jax.ShapeDtypeStruct
    devices = lax.axis_size("ctx")
    heads = lax.axis_size("head")
    length = query_raw.shape[0]
    width = out_weight.shape[1]
    near = [[GROUP * g + i for i in range(GROUP)] for g in range(devices // GROUP)]
    reach = GROUP * ROW
    rows = [
        [z * reach + GROUP * r + i for r in range(ROW)]
        for z in range(devices // reach)
        for i in range(GROUP)
    ]

    def trade(a, groups):
        return lax.all_to_all(a, "ctx", 0, 0, axis_index_groups=groups)

    raw = (query_raw, key_raw, value_raw, query_key_conv, value_conv, beta_logit.T, gate_logit.T)
    fetched = [pltpu.VMEM(raw[i].shape, raw[i].dtype) for i in range(len(raw))]
    message, taps, *rims = call(
        pack_kernel,
        [shape((GROUP, 3 * length + EXTRA, HDIM), BF16), shape((16, HDIM), F32)]
        + [shape((16, 3 * HDIM), BF16)] * GROUP,
        *[in_hbm(a) for a in raw],
        in_hbm(log_rate),
        in_specs=[pl.BlockSpec(memory_space=pltpu.HBM)] * len(raw) + [pl.BlockSpec(memory_space=pltpu.SMEM)],
        scratch_shapes=fetched + [pltpu.SemaphoreType.DMA((len(raw),))],
    )
    rims = [
        lax.ppermute(rim, "ctx", [(i, i + 1 + h) for i in range(GROUP - 1, devices - 1, GROUP)])
        for h, rim in enumerate(rims)
    ]
    message = trade(message, near)
    message, out_weight, output_gate = lax.optimization_barrier((message, out_weight, output_gate))
    maps, own, lifted = call(
        chunk_kernel,
        [
            shape((ROW, 2 * HDIM, HDIM), BF16),
            shape((GROUP * SPAN, HDIM), F32),
            shape((GROUP * SPAN, HDIM), BF16),
        ],
        message,
        taps,
        *rims,
    )
    maps = trade(maps, rows)
    block = shape((HDIM, HDIM), BF16)
    step, add, mine = call(chain_kernel, [block, block, shape((HDIM, 2 * HDIM), F32)], maps)
    states = []
    for slab in range(SLAB - 1):
        leaving = call(relay_kernel, block, step, add, *states) if slab else add
        pairs = [(reach * slab + i, reach * (slab + 1) + i) for i in range(reach)]
        states.append(lax.ppermute(leaving, "ctx", pairs))
    normed = call(
        finish_kernel,
        shape((GROUP, SPAN, HDIM), BF16),
        *states,
        mine,
        own,
        lifted,
        norm_gain.reshape(1, -1),
    )
    normed = trade(normed, near)
    partial = call(project_kernel, shape((length, width), BF16), normed, output_gate, out_weight)
    partial = lax.all_to_all(partial.reshape(heads, length // heads, width), "head", 0, 0)
    return call(sum_kernel, shape(partial.shape[1:], BF16), partial)


def solution(mesh):
    in_specs = (
        P("ctx", "head"),
        P("ctx", "head"),
        P("ctx", "head"),
        P(None, None, "head"),
        P(None, "head"),
        P("ctx", "head"),
        P("ctx", "head"),
        P("ctx", "head"),
        P("head"),
        P(),
        P("head", None),
    )
    out_specs = P(("ctx", "head"), None)
    return jax.shard_map(local, mesh=mesh, in_specs=in_specs, out_specs=out_specs, check_vma=False)
```
